256 devices in a mesh: comp: 4 (over z_lo), dom: 64 (over y, x, z_hi, core).
Axes of the slice: x: 4, y: 4, z: 8 (z_hi: 2, z_lo: 4; z = z_hi * 4 + z_lo), core: 2. Of those that a mesh axis runs over, the one named last changes fastest.
Arguments:
- airside_exchange: bfloat16 [4, 4, 65536], P('comp', None, 'dom'), may hold values from -6 to 6
- regrid_matrix_partitions: bfloat16 [4, 512, 4, 128, 128], P('comp', 'dom'), may hold values from -0.25 to 0.25
- regrid_destination_latitude: int32 [4, 512, 4], P('comp', 'dom'), may hold values from 0 to 2047, all different within a row
- thermal_departure: float32 [32, 2048, 128], P(None, ('comp', 'dom')), may hold values from -6 to 6
- diffusivity_coefficient: float32 [31, 2048, 128], P(None, ('comp', 'dom')), may hold values from 0.05 to 3
- elevation_anomaly_profile: float32 [2048, 128], P(('comp', 'dom')), may hold values from -3 to 3
- depth_integrated_volume_flow: float32 [2, 2048, 128], P(None, ('comp', 'dom')), may hold values from -2 to 2
- marine_indicator: int32 [2048, 128], P(('comp', 'dom')), may hold values 0 or 1
Outputs:
- ocean_temperature: float32 [32, 2048, 128], P(None, ('comp', 'dom'))
- ocean_height: float32 [2048, 128], P(('comp', 'dom'))
- atm_surface: bfloat16 [4, 2, 65536], P('comp', None, 'dom')
The draws below stay inside these ranges and needn't reach their ends.
Inputs may be any that keep to these rules, and one draw needn't show every extreme that they name: `regrid_destination_latitude`: each (section, source block) names 4 different ocean blocks, and every ocean block is named somewhere; ocean block b is grid row b.
All inputs are finite; a program needn't handle non-finite values. No bound on the sum of `marine_indicator` on one device may be relied on, other than what follows from the above.
Results may differ from the reference program's by a relative error of at most 0.0048.
Values may be sent and summed in bfloat16 or wider, within the bound.
No kernel may reach another device: no remote copies, remote signals or barrier semaphores. Data moves between devices by JAX's collectives and lax.ppermute only.
A program may use at most 64 MiB of HBM per device.

```python
import math
import jax
import jax.numpy as jnp
from jax import lax

NF = 4
AC = 1024
BA = 128
MARINE_PATCH_SPAN = 128
K = 4
SB = 8
MARINE_DEPTHS = 32
NSTEP = 2
NSUB = 8
MARINE_LATITUDES = 2048
NSRC = 512
N_COMP = 4
N_DOM = 64


def set_ends(entries, rng, least, high):
    spot = [jax.random.randint(jax.random.fold_in(rng, axis), (), 0, length) for axis, length in enumerate(entries.shape)]
    main_axis = entries.shape.index(max(entries.shape))
    beside = spot[:main_axis] + [(spot[main_axis] + 1) % entries.shape[main_axis]] + spot[main_axis + 1:]
    return entries.at[tuple(spot)].set(least).at[tuple(beside)].set(high)


def block_levels(own_key, dims, shards, low, largest):
    level, own = 1.0, jax.random.fold_in(own_key, 6)
    for position, blocks in shards:
        steps = jnp.exp(jax.random.uniform(jax.random.fold_in(own, position), (blocks,), jnp.float32, low / len(shards), largest / len(shards)))
        level = level * jnp.repeat(steps, dims[position] // blocks).reshape([-1 if axis == position else 1 for axis in range(len(dims))])
    return level


def different_ones(rng, rows, number_of, top, lift):
    sequence = jax.random.permutation(jax.random.fold_in(rng, 1), number_of)
    favour = sequence
    for power in range(3):
        favour = favour * favour // number_of
    favour = favour * lift // number_of
    tickets = jax.random.randint(jax.random.fold_in(rng, 2), (rows, number_of), 0, 4096) + favour
    holders = jax.random.permutation(jax.random.fold_in(rng, 3), rows)[jnp.arange(number_of) % rows]
    tickets = jnp.where(jnp.arange(rows)[:, None] == holders[None, :], 1 << 14, tickets)
    score = tickets * number_of + jnp.arange(number_of)
    return lax.top_k(score.astype(jnp.int32), top)[1].astype(jnp.int32)


def gaussian(own_key, extent, width, limit, pieces=(), kind=jnp.bfloat16):
    values = width * jax.random.normal(own_key, extent, jnp.float32)
    if pieces:
        values = values * block_levels(own_key, extent, pieces, -0.22, 0.18)
    return jnp.clip(values, -limit, limit).astype(kind)


def setup_inputs(seed: int = 0) -> dict:
    arg_keys = jax.random.split(jax.random.key(seed), 9)
    return {
        "airside_exchange": gaussian(arg_keys[0], (N_COMP, NF, N_DOM * AC), 1.0, 6.0, ((0, 4), (2, 64))),
        "regrid_matrix_partitions": gaussian(arg_keys[1], (N_COMP, NSRC, K, BA, MARINE_PATCH_SPAN), (4 * BA) ** -0.5, 0.25, ((0, 4), (1, 64))),
        "regrid_destination_latitude": different_ones(arg_keys[2], N_COMP * NSRC, MARINE_LATITUDES, K, 32).reshape((N_COMP, NSRC, K)),
        "thermal_departure": gaussian(arg_keys[3], (MARINE_DEPTHS, MARINE_LATITUDES, MARINE_PATCH_SPAN), 1.0, 6.0, ((1, 256),), jnp.float32),
        "diffusivity_coefficient": jnp.clip(jnp.exp(math.log(3.0) - 4.0943445 * jax.random.uniform(arg_keys[4], (MARINE_DEPTHS - 1, MARINE_LATITUDES, MARINE_PATCH_SPAN), jnp.float32) ** block_levels(arg_keys[4], (MARINE_DEPTHS - 1, MARINE_LATITUDES, MARINE_PATCH_SPAN), ((1, 256),), -0.2, 0.2)), 0.05, 3.0),
        "elevation_anomaly_profile": gaussian(arg_keys[5], (MARINE_LATITUDES, MARINE_PATCH_SPAN), 0.5, 3.0, ((0, 256),), jnp.float32),
        "depth_integrated_volume_flow": gaussian(arg_keys[6], (2, MARINE_LATITUDES, MARINE_PATCH_SPAN), 0.3, 2.0, ((1, 256),), jnp.float32),
        "marine_indicator": set_ends((jax.random.randint(arg_keys[7], (MARINE_LATITUDES, MARINE_PATCH_SPAN), 0, 10) < 7).astype(jnp.int32), jax.random.fold_in(arg_keys[7], 1), 0, 1),
    }


wave_gain = 0.35
stress_gain = 0.1
fresh_gain = 0.1
spread_gain = 0.2
heating_gain = 0.5


def northward(field):
    return jnp.concatenate([field[..., 1:, :], jnp.zeros_like(field[..., :1, :])], axis=-2)


def southward(field):
    return jnp.concatenate([jnp.zeros_like(field[..., :1, :]), field[..., :-1, :]], axis=-2)


def vertical_solve(explicit, diffusivity_coefficient):
    levels_all = explicit.shape[0]
    solved = []
    ratios = []
    for layer_index in range(levels_all):
        upward = diffusivity_coefficient[layer_index - 1] if layer_index > 0 else jnp.zeros_like(explicit[0])
        downward = diffusivity_coefficient[layer_index] if layer_index < levels_all - 1 else jnp.zeros_like(explicit[0])
        pivots = 1.0 + upward + downward
        if layer_index > 0:
            pivots = pivots - upward * ratios[-1]
            solved.append((explicit[layer_index] + upward * solved[-1]) / pivots)
        else:
            solved.append(explicit[layer_index] / pivots)
        ratios.append(downward / pivots)
    result = [solved[-1]]
    for layer_index in range(levels_all - 2, -1, -1):
        result.append(solved[layer_index] + ratios[layer_index] * result[-1])
    return jnp.stack(result[::-1])


def reference(airside_exchange, regrid_matrix_partitions, regrid_destination_latitude, thermal_departure, diffusivity_coefficient, elevation_anomaly_profile, depth_integrated_volume_flow, marine_indicator):
    sources = airside_exchange.astype(jnp.float32).reshape(N_COMP, NF, N_DOM * SB, BA)
    weights = regrid_matrix_partitions.astype(jnp.float32)
    partial_terms = jnp.einsum("cfra,crkab->crkfb", sources, weights)
    ocean_flux = jnp.zeros((MARINE_LATITUDES, NF, MARINE_PATCH_SPAN), jnp.float32).at[regrid_destination_latitude.reshape(-1)].add(partial_terms.reshape(-1, NF, MARINE_PATCH_SPAN))
    heating = ocean_flux[:, 0, :]
    freshwater = ocean_flux[:, 1, :]
    stress_east = ocean_flux[:, 2, :]
    stress_north = ocean_flux[:, 3, :]
    wet = marine_indicator.astype(jnp.float32)
    face_east = wet * jnp.roll(wet, -1, axis=1)
    face_north = wet * northward(wet)
    height = elevation_anomaly_profile
    flow_east = depth_integrated_volume_flow[0]
    flow_north = depth_integrated_volume_flow[1]
    advected_quantity = thermal_departure
    for outer_step in range(NSTEP):
        for substep in range(NSUB):
            new_east = face_east * (flow_east - wave_gain * (jnp.roll(height, -1, axis=1) - height) + stress_gain * stress_east)
            new_north = face_north * (flow_north - wave_gain * (northward(height) - height) + stress_gain * stress_north)
            height = height - wave_gain * (new_east - jnp.roll(new_east, 1, axis=1) + new_north - southward(new_north)) + fresh_gain * freshwater * wet
            flow_east = new_east
            flow_north = new_north
        along_east = face_east * (jnp.roll(advected_quantity, -1, axis=2) - advected_quantity)
        along_north = face_north * (northward(advected_quantity) - advected_quantity)
        laplace = along_east - jnp.roll(along_east, 1, axis=2) + along_north - southward(along_north)
        explicit = advected_quantity + spread_gain * laplace
        explicit = explicit.at[0].add(heating_gain * heating * wet)
        advected_quantity = vertical_solve(explicit, diffusivity_coefficient)
    surface = jnp.stack([advected_quantity[0], height]).astype(jnp.bfloat16)
    surface = lax.optimization_barrier(surface)
    picked = surface[:, regrid_destination_latitude, :].astype(jnp.float32)
    returned = jnp.einsum("fcrkb,crkab->cfra", picked, weights)
    return advected_quantity, height, returned.reshape(N_COMP, 2, N_DOM * AC).astype(jnp.bfloat16)
```

```python
import numpy as np
import jax
import jax.numpy as jnp
from jax import lax
from jax.experimental import pallas as pl
from jax.experimental.pallas import tpu as pltpu
from jax.sharding import Mesh, PartitionSpec as P

NSTEP = 2
NSUB = 8

wave_gain = 0.35
stress_gain = 0.1
fresh_gain = 0.1
spread_gain = 0.2
heating_gain = 0.5

ALL = ("c", "y", "x", "h", "k")
PLANE = ("y", "x")
LINE = ("c", "h", "k")
ROWS = 8
LANES = 128
LEVELS = 32
TERMS = 32
GROUP = 16
SLAB = 64
BF = jnp.bfloat16
F32 = jnp.float32

vmem = pl.BlockSpec(memory_space=pltpu.VMEM)
smem = pl.BlockSpec(memory_space=pltpu.SMEM)


def call(kernel, outs, ins, scratch=(), name=None):
    return pl.pallas_call(
        kernel,
        out_shape=outs,
        in_specs=ins,
        out_specs=jax.tree.map(lambda _: vmem, outs),
        scratch_shapes=list(scratch),
        name=name,
    )


def shaped(shape, kind):
    return jax.ShapeDtypeStruct(shape, kind)


def east(v):
    return pltpu.roll(v, LANES - 1, axis=v.ndim - 1)


def west(v):
    return pltpu.roll(v, 1, axis=v.ndim - 1)


def north(v):
    return pltpu.roll(v, v.shape[0] - 1, axis=0)


def south(v):
    return pltpu.roll(v, 1, axis=0)


def pack_edges(tracer, mixing, height, flow, wet, up, down, around):
    own = jnp.concatenate([height[...], flow[0], flow[1], wet[...].astype(F32)], axis=0)
    zero = jnp.zeros((1, LANES), F32)
    around[...] = own
    up[0:32] = own
    up[32:64] = tracer[:, ROWS - 2, :]
    up[64:96] = tracer[:, ROWS - 1, :]
    up[96:127] = mixing[:, ROWS - 1, :]
    up[127:128] = zero
    down[0:32] = own
    down[32:64] = tracer[:, 0, :]
    down[64:96] = tracer[:, 1, :]
    down[96:127] = mixing[:, 0, :]
    down[127:128] = zero


def sort_terms(place, received, message, rows_named):
    spot = place[0]
    lines = lax.broadcasted_iota(jnp.int32, (4 * SLAB, LANES), 0)
    line_row = (lines >> 6) * 512 + spot * 32 - 16 + (lines & (SLAB - 1))
    sums = [None] * 4
    for q in range(4):
        coded = sum(received[4 * q + i, 128:144, :].astype(F32) for i in range(4))
        named = coded[0:1] * 64.0 + coded[1:2]
        rows_named[q : q + 1, :] = named
        picks = jnp.where(line_row == named.astype(jnp.int32), 1.0, 0.0).astype(BF)
        for f in range(4):
            some = received[4 * q : 4 * q + 4, f * 32 : f * 32 + 32, :].reshape(LANES, LANES)
            part = jnp.dot(picks, some, preferred_element_type=F32)
            sums[f] = part if sums[f] is None else sums[f] + part
    for c in range(4):
        for s in range(4):
            base = c * SLAB + 16 + s * ROWS
            pieces = [
                sums[f][base + o : base + o + ROWS] for f in (1, 2, 3) for o in (0, 8, 16, -16, -8)
            ] + [sums[0][base + o : base + o + ROWS] for o in (0, 8, -8)]
            message[c * 4 + s] = jnp.concatenate(pieces, axis=0).astype(BF)


def first_step(tracer, mixing, wet_own, before, after, base, reply, factors, halo, mix_halo, work):
    halo[...] = jnp.zeros_like(halo)
    mix_halo[...] = jnp.zeros_like(mix_halo)
    halo[pl.ds(0, LEVELS, stride=ROWS), :] = after[32:64]
    halo[pl.ds(1, LEVELS, stride=ROWS), :] = after[64:96]
    halo[pl.ds(6, LEVELS, stride=ROWS), :] = before[32:64]
    halo[pl.ds(7, LEVELS, stride=ROWS), :] = before[64:96]
    mix_halo[pl.ds(0, LEVELS, stride=ROWS), :] = after[96:128]
    mix_halo[pl.ds(7, LEVELS, stride=ROWS), :] = before[96:128]
    lower = lax.broadcasted_iota(jnp.int32, (ROWS, LANES), 0) < 4
    wet = jnp.concatenate(
        [wet_own[...].astype(F32), jnp.where(lower, after[24:32], before[24:32])], axis=0
    )
    face_e = wet * east(wet)
    face_n = wet * north(wet)
    face_w = west(face_e)
    face_s = south(face_n)

    def level(ref, own, l):
        return jnp.concatenate([own[l], ref[l * ROWS : (l + 1) * ROWS, :]], axis=0)

    zero = jnp.zeros((2 * ROWS, LANES), F32)
    over, ratio, solved, gone = zero, zero, zero, zero
    for l in range(LEVELS):
        t = level(halo, tracer, l)
        explicit = t + spread_gain * (
            face_e * (east(t) - t)
            - face_w * (t - west(t))
            + face_n * (north(t) - t)
            - face_s * (t - south(t))
        )
        under = level(mix_halo, mixing, l) if l < LEVELS - 1 else zero
        inverse = 1.0 / (1.0 + under + over * (1.0 - ratio))
        carry = over * inverse
        ratio = under * inverse
        solved = explicit * inverse + carry * solved
        gone = carry * gone if l else inverse
        factors[0, l] = inverse[0:ROWS]
        factors[1, l] = carry[0:ROWS]
        factors[2, l] = ratio[0:ROWS]
        work[l] = ratio
        base[l] = solved
        reply[l] = gone
        over = under
    for l in range(LEVELS - 2, -1, -1):
        solved = base[l] + work[l] * solved
        gone = reply[l] + work[l] * gone
        base[l] = solved
        reply[l] = gone


def ocean(
    flux, height, flow, wet_own, before2, before, after, after2, base, reply, factors,
    tracer_out, height_out, message, work,
):
    def ring(i, own):
        r = slice(i * ROWS, (i + 1) * ROWS)
        return jnp.concatenate([own, after[r], after2[r], before2[r], before[r]], axis=0)

    total = flux[0].astype(F32)
    for p in range(1, GROUP):
        total = total + flux[p].astype(F32)
    wet = ring(3, wet_own[...].astype(F32))
    rain = fresh_gain * total[0:40] * wet
    push_e = stress_gain * total[40:80]
    push_n = stress_gain * total[80:120]
    h = ring(0, height[...])
    flow_e = ring(1, flow[0])
    flow_n = ring(2, flow[1])
    face_e = wet * east(wet)
    face_n = wet * north(wet)
    face_w, flow_w, push_w = west(face_e), west(flow_e), west(push_e)
    face_s, flow_s, push_s = south(face_n), south(flow_n), south(push_n)
    for _ in range(NSTEP * NSUB):
        flow_e = face_e * (flow_e - wave_gain * (east(h) - h) + push_e)
        flow_w = face_w * (flow_w - wave_gain * (h - west(h)) + push_w)
        flow_n = face_n * (flow_n - wave_gain * (north(h) - h) + push_n)
        flow_s = face_s * (flow_s - wave_gain * (h - south(h)) + push_s)
        h = h - wave_gain * (flow_e - flow_w + flow_n - flow_s) + rain
    height_out[...] = h[0:ROWS]

    wet16 = jnp.concatenate([wet[0:ROWS], jnp.where(
        lax.broadcasted_iota(jnp.int32, (ROWS, LANES), 0) < 4, wet[8:16], wet[32:40])], axis=0)
    heat = jnp.concatenate([total[120:128], jnp.where(
        lax.broadcasted_iota(jnp.int32, (ROWS, LANES), 0) < 4, total[128:136], total[136:144])], axis=0)
    warm = heating_gain * heat * wet16
    fe, fw, fn, fs = face_e[0:ROWS], face_w[0:ROWS], face_n[0:ROWS], face_s[0:ROWS]
    solved = None
    for l in range(LEVELS):
        both = base[l] + reply[l] * warm
        t = both[0:ROWS]
        explicit = t + spread_gain * (
            fe * (east(t) - t)
            - fw * (t - west(t))
            + fn * (north(both)[0:ROWS] - t)
            - fs * (t - south(both)[0:ROWS])
        )
        if l == 0:
            explicit = explicit + warm[0:ROWS]
            solved = explicit * factors[0, l]
        else:
            solved = explicit * factors[0, l] + factors[1, l] * solved
        work[l] = solved
    tracer_out[LEVELS - 1] = solved
    for l in range(LEVELS - 2, -1, -1):
        solved = work[l] + factors[2, l] * solved
        tracer_out[l] = solved
    top = jnp.concatenate([solved, h[0:ROWS]], axis=0).astype(BF)
    for p in range(GROUP):
        message[p] = top


def answer(place, rows_named, received, message):
    spot = place[0]
    have = received[...].reshape(GROUP * 16, LANES)
    lines = lax.broadcasted_iota(jnp.int32, (GROUP * 16, LANES), 0)
    line_row = (lines >> 6) * 512 + spot * 32 + ((lines >> 4) & 3) * ROWS + (lines & 7)
    second = (lines & 8) != 0
    for q in range(4):
        named = rows_named[q : q + 1, :].astype(jnp.int32)
        same = line_row == named
        for f in range(2):
            picks = jnp.where(same & (second == bool(f)), 1.0, 0.0).astype(BF)
            out = lax.dot_general(
                picks, have, (((0,), (0,)), ((), ())), preferred_element_type=F32
            ).astype(BF)
            message[4 * q : 4 * q + 4, f * 32 : f * 32 + 32, :] = out.reshape(4, 32, LANES)


def collect(received, chosen):
    total = received[0].astype(F32)
    for p in range(1, GROUP):
        total = total + received[p].astype(F32)
    chosen[...] = total.astype(BF)


def shards(airside, matrices, latitude, tracer, mixing, height, flow, marine):
    sources = airside[0].reshape(4, 8, LANES)
    weights = matrices[0]
    targets = latitude[0].reshape(-1)
    spot = lax.axis_index(PLANE)
    place = spot.astype(jnp.int32).reshape(1)
    count = lax.axis_size(ALL)

    up, down, around = call(
        pack_edges,
        (shaped((128, LANES), F32), shaped((128, LANES), F32), shaped((32, LANES), F32)),
        [vmem] * 5,
        name="pack_edges",
    )(tracer, mixing, height, flow, marine)

    def moved(value, step):
        pairs = [(i, i + step) for i in range(count) if 0 <= i + step < count]
        return lax.ppermute(value, ALL, pairs)

    before = moved(up, 1)
    after = moved(down, -1)
    before2 = moved(around, 2)
    after2 = moved(around, -2)

    terms = jnp.einsum("fsa,skab->fskb", sources, weights, preferred_element_type=F32)
    terms = terms.astype(BF).reshape(128, LANES)
    lanes = jnp.arange(LANES, dtype=jnp.int32)
    spread = jnp.where(lanes // TERMS == spot % 4, jnp.tile(targets, 4), 0)
    coded = jnp.stack([spread // 64, spread % 64]).astype(BF)
    coded = jnp.concatenate([coded, jnp.zeros((14, LANES), BF)])
    first = jnp.concatenate([terms, coded])
    first = jnp.broadcast_to(first[None], (GROUP, 144, LANES))
    first = lax.all_to_all(first, PLANE, 0, 0, tiled=True)

    second, rows_named = call(
        sort_terms,
        (shaped((GROUP, 144, LANES), BF), shaped((ROWS, LANES), F32)),
        [smem, vmem],
        name="sort_terms",
    )(place, first)
    second = lax.all_to_all(second, LINE, 0, 0, tiled=True)

    base, reply, factors = call(
        first_step,
        (
            shaped((LEVELS, 2 * ROWS, LANES), F32),
            shaped((LEVELS, 2 * ROWS, LANES), F32),
            shaped((3, LEVELS, ROWS, LANES), F32),
        ),
        [vmem] * 5,
        [
            pltpu.VMEM((LEVELS * ROWS, LANES), F32),
            pltpu.VMEM((LEVELS * ROWS, LANES), F32),
            pltpu.VMEM((LEVELS, 2 * ROWS, LANES), F32),
        ],
        name="first_step",
    )(tracer, mixing, marine, before, after)

    tracer_new, height_new, third = call(
        ocean,
        (
            shaped((LEVELS, ROWS, LANES), F32),
            shaped((ROWS, LANES), F32),
            shaped((GROUP, 16, LANES), BF),
        ),
        [vmem] * 11,
        [pltpu.VMEM((LEVELS, ROWS, LANES), F32)],
        name="ocean",
    )(second, height, flow, marine, before2, before, after, after2, base, reply, factors)
    third = lax.all_to_all(third, LINE, 0, 0, tiled=True)

    fourth = call(
        answer, shaped((GROUP, 64, LANES), BF), [smem, vmem, vmem], name="answer"
    )(place, rows_named, third)
    fourth = lax.all_to_all(fourth, PLANE, 0, 0, tiled=True)

    chosen = call(collect, shaped((64, LANES), BF), [vmem], name="collect")(fourth)
    returned = jnp.einsum(
        "fskb,skab->fsa", chosen.reshape(2, 8, 4, LANES), weights, preferred_element_type=F32
    )
    return tracer_new, height_new, returned.reshape(1, 2, 8 * LANES).astype(BF)


def solution(mesh):
    split = Mesh(mesh.devices.reshape(4, 4, 4, 2, 2), ALL)
    dom = ("y", "x", "h", "k")
    return jax.shard_map(
        shards,
        mesh=split,
        in_specs=(
            P("c", None, dom),
            P("c", dom, None, None, None),
            P("c", dom, None),
            P(None, ALL, None),
            P(None, ALL, None),
            P(ALL, None),
            P(None, ALL, None),
            P(ALL, None),
        ),
        out_specs=(P(None, ALL, None), P(ALL, None), P("c", None, dom)),
        check_vma=False,
    )
```

```python
import numpy as np
import jax
import jax.numpy as jnp
from jax import lax
from jax.experimental import pallas as pl
from jax.experimental.pallas import tpu as pltpu
from jax.sharding import Mesh, PartitionSpec as P

NSTEP = 2
NSUB = 8

wave_gain = 0.35
stress_gain = 0.1
fresh_gain = 0.1
spread_gain = 0.2
heating_gain = 0.5

ALL = ("c", "y", "x", "h", "k")
PLANE = ("y", "x")
LINE = ("c", "h", "k")
ROWS = 8
LANES = 128
LEVELS = 32
TERMS = 32
GROUP = 16
SLAB = 64
BF = jnp.bfloat16
F32 = jnp.float32

vmem = pl.BlockSpec(memory_space=pltpu.VMEM)
smem = pl.BlockSpec(memory_space=pltpu.SMEM)


def call(kernel, outs, ins, scratch=(), name=None):
    return pl.pallas_call(
        kernel,
        out_shape=outs,
        in_specs=ins,
        out_specs=jax.tree.map(lambda _: vmem, outs),
        scratch_shapes=list(scratch),
        name=name,
    )


def shaped(shape, kind):
    return jax.ShapeDtypeStruct(shape, kind)


def inside(shape, kind):
    return pltpu.VMEM(shape, kind)


def near(value):
    return pltpu.with_memory_space_constraint(value, pltpu.VMEM)


def east(v):
    return pltpu.roll(v, LANES - 1, axis=v.ndim - 1)


def west(v):
    return pltpu.roll(v, 1, axis=v.ndim - 1)


def north(v):
    return pltpu.roll(v, v.shape[0] - 1, axis=0)


def south(v):
    return pltpu.roll(v, 1, axis=0)


def pack_edges(quarter, tracer, mixing, height, flow, wet, edges, leaving):
    own = jnp.concatenate([height[...], flow[0], flow[1], wet[...].astype(F32)], axis=0).astype(BF)
    zero = jnp.zeros((1, LANES), F32)
    for i, (first, second, rim) in enumerate(((6, 7, 7), (0, 1, 0))):
        edges[i, 0:32] = own
        edges[i, 32:64] = tracer[:, first, :].astype(BF)
        edges[i, 64:96] = tracer[:, second, :].astype(BF)
        edges[i, 96:128] = jnp.concatenate([mixing[:, rim, :], zero], axis=0).astype(BF)
    leaving[...] = edges[jnp.where(quarter[0] >= 2, 0, 1)]


def pair_edges(quarter, edges, arrived, _after, message):
    mine = quarter[0]
    message[0:32] = edges[0, 0:32]
    message[32:64] = arrived[0:32]
    message[64:160] = edges[mine & 1, 32:128]

    @pl.when(mine == 1)
    def _():
        message[160:256] = edges[0, 32:128]

    @pl.when(mine == 2)
    def _():
        message[160:256] = edges[1, 32:128]

    @pl.when((mine == 0) | (mine == 3))
    def _():
        message[160:256] = arrived[32:128]


def far_edges(quarter, edges, arrived, partner, message):
    core = quarter[0] & 1
    own = pl.multiple_of(32 * core, 32)
    other = pl.multiple_of(32 - 32 * core, 32)
    message[pl.ds(own, 32)] = edges[0, 0:32]
    message[pl.ds(other, 32)] = partner[0:32]
    message[pl.ds(64 + own, 32)] = arrived[0:32]
    message[pl.ds(64 + other, 32)] = partner[32:64]
    message[128:224] = partner[160:256]


def edge_sides(mine, partner, far):
    first = (mine & 1) == 0
    near_edge = partner[64:160].astype(F32)
    far_edge = far[128:224].astype(F32)
    return jnp.where(first, far_edge, near_edge), jnp.where(first, near_edge, far_edge)


def strips(mine, partner, far):
    first = (mine & 1) == 0
    shift = 32 * (mine & 1)
    prev = jnp.where(mine < 2, 64, 0)
    follow = 64 - prev

    def part(start):
        return far[pl.ds(pl.multiple_of(start, 32), 32)].astype(F32)

    beside = partner[0:32].astype(F32)
    before2 = part(prev + shift)
    before = jnp.where(first, part(prev + 32), beside)
    after = jnp.where(first, beside, part(follow))
    after2 = part(follow + shift)
    return before2, before, after, after2


def sort_terms(place, received, _arrived, message, rows_named):
    spot = place[0]
    lines = lax.broadcasted_iota(jnp.int32, (4 * SLAB, LANES), 0)
    line_row = (lines >> 6) * 512 + spot * 32 - 16 + (lines & (SLAB - 1))
    sums = [None] * 4
    tile = lax.broadcasted_iota(jnp.int32, (ROWS, LANES), 0)
    head, last = tile == 0, tile == ROWS - 1
    for q in range(4):
        coded = sum(received[4 * q + i, 128:144, :].astype(F32) for i in range(4))
        named = coded[0:1] * 64.0 + coded[1:2]
        rows_named[q : q + 1, :] = named
        picks = jnp.where(line_row == named.astype(jnp.int32), 1.0, 0.0).astype(BF)
        for f in range(4):
            some = received[4 * q : 4 * q + 4, f * 32 : f * 32 + 32, :].reshape(LANES, LANES)
            part = jnp.dot(picks, some, preferred_element_type=F32)
            sums[f] = part if sums[f] is None else sums[f] + part
    for c in range(4):
        for s in range(4):
            base = c * SLAB + 16 + s * ROWS
            pieces = []
            for f in (1, 2, 3):
                for o in (0, 8, 16, -16, -8):
                    piece = sums[f][base + o : base + o + ROWS]
                    if f == 1 and o == 16:
                        piece = jnp.where(last, north(sums[0][base + 8 : base + 16]), piece)
                    if f == 1 and o == -16:
                        piece = jnp.where(head, south(sums[0][base - 8 : base]), piece)
                    pieces.append(piece)
            pieces.append(sums[0][base : base + ROWS])
            message[c * 4 + s] = jnp.concatenate(pieces, axis=0).astype(BF)


def first_step(quarter, tracer, mixing, wet_own, partner, far, base, reply, factors, halo, mix_halo, work):
    mine = quarter[0]
    before, after = edge_sides(mine, partner, far)
    _, wet_before, wet_after, _ = (strip[24:32] for strip in strips(mine, partner, far))
    halo[...] = jnp.zeros_like(halo)
    mix_halo[...] = jnp.zeros_like(mix_halo)
    halo[pl.ds(0, LEVELS, stride=ROWS), :] = after[0:32]
    halo[pl.ds(1, LEVELS, stride=ROWS), :] = after[32:64]
    halo[pl.ds(6, LEVELS, stride=ROWS), :] = before[0:32]
    halo[pl.ds(7, LEVELS, stride=ROWS), :] = before[32:64]
    mix_halo[pl.ds(0, LEVELS, stride=ROWS), :] = after[64:96]
    mix_halo[pl.ds(7, LEVELS, stride=ROWS), :] = before[64:96]
    lower = lax.broadcasted_iota(jnp.int32, (ROWS, LANES), 0) < 4
    wet = jnp.concatenate(
        [wet_own[...].astype(F32), jnp.where(lower, wet_after, wet_before)], axis=0
    )
    face_e = wet * east(wet)
    face_n = wet * north(wet)
    face_w = west(face_e)
    face_s = south(face_n)

    def level(ref, own, l):
        return jnp.concatenate([own[l], ref[l * ROWS : (l + 1) * ROWS, :]], axis=0)

    zero = jnp.zeros((2 * ROWS, LANES), F32)
    over, ratio, solved, gone = zero, zero, zero, zero
    for l in range(LEVELS):
        t = level(halo, tracer, l)
        explicit = t + spread_gain * (
            face_e * (east(t) - t)
            - face_w * (t - west(t))
            + face_n * (north(t) - t)
            - face_s * (t - south(t))
        )
        under = level(mix_halo, mixing, l) if l < LEVELS - 1 else zero
        inverse = 1.0 / (1.0 + under + over * (1.0 - ratio))
        carry = over * inverse
        ratio = under * inverse
        solved = explicit * inverse + carry * solved
        gone = carry * gone if l else inverse
        factors[0, l] = inverse[0:ROWS]
        factors[1, l] = carry[0:ROWS]
        factors[2, l] = ratio[0:ROWS]
        work[l] = ratio
        base[l] = solved
        reply[l] = gone
        over = under
    for l in range(LEVELS - 2, -1, -1):
        solved = base[l] + work[l] * solved
        gone = reply[l] + work[l] * gone
        base[l] = solved
        reply[l] = gone


def ocean(
    quarter, flux, height, flow, wet_own, partner, far, base, reply, factors,
    tracer_out, height_out, message, work,
):
    mine = quarter[0]
    before2, before, after, after2 = strips(mine, partner, far)

    def ring(i, own):
        r = slice(i * ROWS, (i + 1) * ROWS)
        return jnp.concatenate([own, after[r], after2[r], before2[r], before[r]], axis=0)

    total = flux[0].astype(F32)
    for p in range(1, GROUP):
        total = total + flux[p].astype(F32)
    wet = ring(3, wet_own[...].astype(F32))
    rain = fresh_gain * total[0:40] * wet
    push_e = stress_gain * total[40:80]
    push_n = stress_gain * total[80:120]
    h = ring(0, height[...])
    flow_e = ring(1, flow[0])
    flow_n = ring(2, flow[1])
    face_e = wet * east(wet)
    face_n = wet * north(wet)
    face_w, flow_w, push_w = west(face_e), west(flow_e), west(push_e)
    face_s, flow_s, push_s = south(face_n), south(flow_n), south(push_n)
    for _ in range(NSTEP * NSUB):
        flow_e = face_e * (flow_e - wave_gain * (east(h) - h) + push_e)
        flow_w = face_w * (flow_w - wave_gain * (h - west(h)) + push_w)
        flow_n = face_n * (flow_n - wave_gain * (north(h) - h) + push_n)
        flow_s = face_s * (flow_s - wave_gain * (h - south(h)) + push_s)
        h = h - wave_gain * (flow_e - flow_w + flow_n - flow_s) + rain
    height_out[...] = h[0:ROWS]

    wet16 = jnp.concatenate([wet[0:ROWS], jnp.where(
        lax.broadcasted_iota(jnp.int32, (ROWS, LANES), 0) < 4, wet[8:16], wet[32:40])], axis=0)
    tile = lax.broadcasted_iota(jnp.int32, (ROWS, LANES), 0)
    after_heat = jnp.where(tile == 0, south(total[16:24]), 0.0)
    before_heat = jnp.where(tile == ROWS - 1, north(total[24:32]), 0.0)
    heat = jnp.concatenate([total[120:128], after_heat + before_heat], axis=0)
    warm = heating_gain * heat * wet16
    fe, fw, fn, fs = face_e[0:ROWS], face_w[0:ROWS], face_n[0:ROWS], face_s[0:ROWS]
    solved = None
    for l in range(LEVELS):
        both = base[l] + reply[l] * warm
        t = both[0:ROWS]
        explicit = t + spread_gain * (
            fe * (east(t) - t)
            - fw * (t - west(t))
            + fn * (north(both)[0:ROWS] - t)
            - fs * (t - south(both)[0:ROWS])
        )
        if l == 0:
            explicit = explicit + warm[0:ROWS]
            solved = explicit * factors[0, l]
        else:
            solved = explicit * factors[0, l] + factors[1, l] * solved
        work[l] = solved
    tracer_out[LEVELS - 1] = solved
    for l in range(LEVELS - 2, -1, -1):
        solved = work[l] + factors[2, l] * solved
        tracer_out[l] = solved
    top = jnp.concatenate([solved, h[0:ROWS]], axis=0).astype(BF)
    for p in range(GROUP):
        message[p] = top


def answer(place, rows_named, received, message):
    spot = place[0]
    have = received[...].reshape(GROUP * 16, LANES)
    lines = lax.broadcasted_iota(jnp.int32, (GROUP * 16, LANES), 0)
    line_row = (lines >> 6) * 512 + spot * 32 + ((lines >> 4) & 3) * ROWS + (lines & 7)
    second = (lines & 8) != 0
    for q in range(4):
        named = rows_named[q : q + 1, :].astype(jnp.int32)
        same = line_row == named
        for f in range(2):
            picks = jnp.where(same & (second == bool(f)), 1.0, 0.0).astype(BF)
            out = lax.dot_general(
                picks, have, (((0,), (0,)), ((), ())), preferred_element_type=F32
            ).astype(BF)
            message[4 * q : 4 * q + 4, f * 32 : f * 32 + 32, :] = out.reshape(4, 32, LANES)


def collect(received, chosen):
    total = received[0].astype(F32)
    for p in range(1, GROUP):
        total = total + received[p].astype(F32)
    chosen[...] = total.astype(BF)


def shards(airside, matrices, latitude, tracer, mixing, height, flow, marine):
    sources = airside[0].reshape(4, 8, LANES)
    weights = matrices[0]
    targets = latitude[0].reshape(-1)
    spot = lax.axis_index(PLANE)
    place = spot.astype(jnp.int32).reshape(1)
    count = lax.axis_size(ALL)

    quarter = lax.axis_index(("h", "k")).astype(jnp.int32).reshape(1)
    edges, leaving = call(
        pack_edges,
        (inside((2, 128, LANES), BF), inside((128, LANES), BF)),
        [smem] + [vmem] * 5,
        name="pack_edges",
    )(quarter, tracer, mixing, height, flow, marine)
    pairs = []
    for i in range(count):
        j = i + 4 if i % 4 >= 2 else i - 4
        if 0 <= j < count:
            pairs.append((i, j))
    arrived = near(lax.ppermute(leaving, ALL, pairs))
    edges = near(edges)

    terms = jnp.einsum("fsa,skab->fskb", sources, weights, preferred_element_type=F32)
    terms = terms.astype(BF).reshape(128, LANES)
    lanes = jnp.arange(LANES, dtype=jnp.int32)
    spread = jnp.where(lanes // TERMS == spot % 4, jnp.tile(targets, 4), 0)
    coded = jnp.stack([spread // 64, spread % 64]).astype(BF)
    coded = jnp.concatenate([coded, jnp.zeros((14, LANES), BF)])
    first = jnp.concatenate([terms, coded])
    first = jnp.broadcast_to(first[None], (GROUP, 144, LANES))
    first = near(lax.all_to_all(first, PLANE, 0, 0, tiled=True))

    second, rows_named = call(
        sort_terms,
        (inside((GROUP, 128, LANES), BF), inside((ROWS, LANES), F32)),
        [smem, vmem, vmem],
        name="sort_terms",
    )(place, first, arrived)
    rows_named = near(rows_named)
    second = near(lax.all_to_all(second, LINE, 0, 0, tiled=True))

    partner = call(
        pair_edges, inside((256, LANES), BF), [smem, vmem, vmem, vmem], name="pair_edges"
    )(quarter, edges, arrived, rows_named)
    partner = near(lax.ppermute(partner, ALL, [(i, i ^ 1) for i in range(count)]))
    far = call(
        far_edges, inside((224, LANES), BF), [smem, vmem, vmem, vmem], name="far_edges"
    )(quarter, edges, arrived, partner)
    far = near(lax.ppermute(far, ALL, [(i, i ^ 2) for i in range(count)]))

    base, reply, factors = call(
        first_step,
        (
            inside((LEVELS, 2 * ROWS, LANES), F32),
            inside((LEVELS, 2 * ROWS, LANES), F32),
            inside((3, LEVELS, ROWS, LANES), F32),
        ),
        [smem] + [vmem] * 5,
        [
            pltpu.VMEM((LEVELS * ROWS, LANES), F32),
            pltpu.VMEM((LEVELS * ROWS, LANES), F32),
            pltpu.VMEM((LEVELS, 2 * ROWS, LANES), F32),
        ],
        name="first_step",
    )(quarter, tracer, mixing, marine, partner, far)

    tracer_new, height_new, third = call(
        ocean,
        (
            shaped((LEVELS, ROWS, LANES), F32),
            shaped((ROWS, LANES), F32),
            inside((GROUP, 16, LANES), BF),
        ),
        [smem] + [vmem] * 9,
        [pltpu.VMEM((LEVELS, ROWS, LANES), F32)],
        name="ocean",
    )(quarter, second, height, flow, marine, partner, far, near(base), near(reply), near(factors))
    third = near(lax.all_to_all(third, LINE, 0, 0, tiled=True))

    fourth = call(
        answer, inside((GROUP, 64, LANES), BF), [smem, vmem, vmem], name="answer"
    )(place, rows_named, third)
    fourth = near(lax.all_to_all(fourth, PLANE, 0, 0, tiled=True))

    chosen = call(collect, inside((64, LANES), BF), [vmem], name="collect")(fourth)
    returned = jnp.einsum(
        "fskb,skab->fsa", chosen.reshape(2, 8, 4, LANES), weights, preferred_element_type=F32
    )
    return tracer_new, height_new, returned.reshape(1, 2, 8 * LANES).astype(BF)


def solution(mesh):
    split = Mesh(mesh.devices.reshape(4, 4, 4, 2, 2), ALL)
    dom = ("y", "x", "h", "k")
    return jax.shard_map(
        shards,
        mesh=split,
        in_specs=(
            P("c", None, dom),
            P("c", dom, None, None, None),
            P("c", dom, None),
            P(None, ALL, None),
            P(None, ALL, None),
            P(ALL, None),
            P(None, ALL, None),
            P(ALL, None),
        ),
        out_specs=(P(None, ALL, None), P(ALL, None), P("c", None, dom)),
        check_vma=False,
    )
```

```python
import jax
import jax.numpy as jnp
from jax import lax
from jax.experimental import pallas as pl
from jax.experimental.pallas import tpu as pltpu
from jax.sharding import Mesh, PartitionSpec as P

NSTEP = 2
NSUB = 8

wave_gain = 0.35
stress_gain = 0.1
fresh_gain = 0.1
spread_gain = 0.2
heating_gain = 0.5

ALL = ("c", "y", "x", "h", "k")
PLANE = ("y", "x")
LINE = ("c", "h", "k")
ROWS = 8
LANES = 128
LEVELS = 32
TERMS = 32
GROUP = 16
SLAB = 64
BF = jnp.bfloat16
F32 = jnp.float32

vmem = pl.BlockSpec(memory_space=pltpu.VMEM)
smem = pl.BlockSpec(memory_space=pltpu.SMEM)
far = pl.BlockSpec(memory_space=pltpu.HBM)


def call(kernel, outs, ins, scratch=(), out_specs=None, room=12 << 10):
    return pl.pallas_call(
        kernel,
        out_shape=outs,
        in_specs=ins,
        out_specs=jax.tree.map(lambda _: vmem, outs) if out_specs is None else out_specs,
        scratch_shapes=list(scratch),
        compiler_params=pltpu.CompilerParams(vmem_limit_bytes=room << 10),
    )


def shaped(shape, kind):
    return jax.ShapeDtypeStruct(shape, kind)


def inside(shape, kind):
    return pltpu.VMEM(shape, kind)


def near(value):
    return pltpu.with_memory_space_constraint(value, pltpu.VMEM)


def east(v):
    return pltpu.roll(v, LANES - 1, axis=v.ndim - 1)


def west(v):
    return pltpu.roll(v, 1, axis=v.ndim - 1)


def north(v):
    return pltpu.roll(v, v.shape[0] - 1, axis=0)


def south(v):
    return pltpu.roll(v, 1, axis=0)


def prepare(
    place, quarter, tracer_far, mixing_far, height_far, flow_far, wet_far, targets_far, sources_far,
    weights_far, leaving, both, own, weights, message,
    tracer, mixing, wet, targets, sources, flat, packet, done,
):
    def load(source, target, i):
        copy = pltpu.make_async_copy(source, target, done.at[i])
        copy.start()
        return copy

    edges = [
        load(tracer_far, tracer, 0),
        load(mixing_far, mixing, 1),
        load(height_far, own.at[0:8], 2),
        load(flow_far.at[0], own.at[8:16], 3),
        load(flow_far.at[1], own.at[16:24], 4),
        load(wet_far, wet, 5),
    ]
    small = [load(targets_far, targets, 6), load(sources_far, sources, 7)]
    large = [load(weights_far.at[s], weights.at[s], 8 + s) for s in range(8)]
    for copy in edges:
        copy.wait()
    own[24:32] = wet[...].astype(F32)
    zero = jnp.zeros((1, LANES), F32)
    for i, (first, second, rim) in enumerate(((6, 7, 7), (0, 1, 0))):
        both[i, 0:32] = tracer[:, first, :].astype(BF)
        both[i, 32:64] = tracer[:, second, :].astype(BF)
        both[i, 64:96] = jnp.concatenate([mixing[:, rim, :], zero], axis=0).astype(BF)
    leaving[0:32] = own[...].astype(BF)
    leaving[32:128] = both[jnp.where(quarter[0] >= 2, 0, 1)]
    for copy in small:
        copy.wait()
    lane = lax.broadcasted_iota(jnp.int32, (4, LANES), 1)
    link = lax.broadcasted_iota(jnp.int32, (4, LANES), 0)
    mine = (lane >> 5 == (place[0] & 3)) & ((lane & 3) == link)
    named = jnp.zeros((4, LANES), jnp.int32)
    for s in range(8):
        column = jnp.broadcast_to(targets[:, s : s + 1], (4, LANES))
        named = named + jnp.where(mine & ((lane & 31) >> 2 == s), column, 0)
    named = jnp.broadcast_to(jnp.sum(named, axis=0, keepdims=True), (ROWS, LANES))
    line = lax.broadcasted_iota(jnp.int32, (ROWS, LANES), 0)
    coded = jnp.where(line == 0, named >> 6, jnp.where(line == 1, named & 63, 0)).astype(F32)
    coded = jnp.concatenate([coded, jnp.zeros((ROWS, LANES), F32)], axis=0).astype(BF)
    packet[128:144] = coded
    blank = jnp.zeros((4, LANES), F32)
    for s in range(0, 8, 2):
        some = [sources[:, i * LANES : (i + 1) * LANES].astype(F32) for i in (s, s + 1)]
        left = jnp.concatenate(
            [
                jnp.concatenate([some[0], blank], axis=1),
                jnp.concatenate([blank, some[1]], axis=1),
            ],
            axis=0,
        ).astype(BF)
        large[s].wait()
        large[s + 1].wait()
        for k in (0, 2):
            right = jnp.concatenate(
                [
                    jnp.concatenate([weights[i, k], weights[i, k + 1]], axis=1)
                    for i in (s, s + 1)
                ],
                axis=0,
            )
            out = jnp.dot(left, right, preferred_element_type=F32)
            for i in range(2):
                for j in range(2):
                    flat[pl.ds((s + i) * 4 + k + j, 4, stride=TERMS), :] = out[
                        4 * i : 4 * i + 4, j * LANES : (j + 1) * LANES
                    ]
    packet[0:128] = flat[...].astype(BF)
    sent = [load(packet, message.at[p], p) for p in range(GROUP)]
    for copy in sent:
        copy.wait()


def quad_edges(quarter, leaving, both, arrived, message):
    mine = quarter[0]
    message[0:32] = leaving[0:32]
    message[32:64] = arrived[0:32]
    ends = (mine == 0) | (mine == 3)

    @pl.when(ends)
    def _():
        message[64:160] = arrived[32:128]

    @pl.when(jnp.logical_not(ends))
    def _():
        message[64:160] = both[(mine + 1) & 1]


def pair_edges(quarter, leaving, both, opposite, _after, message):
    message[0:32] = leaving[0:32]
    message[32:96] = opposite[0:64]
    message[96:192] = both[quarter[0] & 1]
    message[192:288] = opposite[64:160]


def edge_sides(mine, partner):
    first = (mine & 1) == 0
    near_edge = partner[96:192].astype(F32)
    far_edge = partner[192:288].astype(F32)
    return jnp.where(first, far_edge, near_edge), jnp.where(first, near_edge, far_edge)


def strips(mine, opposite, partner):
    first = (mine & 1) == 0
    low = mine < 2
    beside = partner[0:32].astype(F32)
    ours = (opposite[0:32].astype(F32), opposite[32:64].astype(F32))
    theirs = (partner[32:64].astype(F32), partner[64:96].astype(F32))
    prev_own = jnp.where(low, ours[1], ours[0])
    prev_other = jnp.where(low, theirs[1], theirs[0])
    next_own = jnp.where(low, ours[0], ours[1])
    next_other = jnp.where(low, theirs[0], theirs[1])
    before2 = prev_own
    before = jnp.where(first, prev_other, beside)
    after = jnp.where(first, beside, next_other)
    after2 = next_own
    return before2, before, after, after2


def sort_terms(place, received, _arrived, message, rows_named):
    spot = place[0]
    lines = lax.broadcasted_iota(jnp.int32, (4 * SLAB, LANES), 0)
    line_row = (lines >> 6) * 512 + spot * 32 - 16 + (lines & (SLAB - 1))
    sums = [None] * 4
    tile = lax.broadcasted_iota(jnp.int32, (ROWS, LANES), 0)
    head, last = tile == 0, tile == ROWS - 1
    for q in range(4):
        coded = sum(received[4 * q + i, 128:144, :].astype(F32) for i in range(4))
        named = coded[0:1] * 64.0 + coded[1:2]
        rows_named[q : q + 1, :] = named
        picks = jnp.where(line_row == named.astype(jnp.int32), 1.0, 0.0).astype(BF)
        for f in range(4):
            some = received[4 * q : 4 * q + 4, f * 32 : f * 32 + 32, :].reshape(LANES, LANES)
            part = jnp.dot(picks, some, preferred_element_type=F32)
            sums[f] = part if sums[f] is None else sums[f] + part
    for c in range(4):
        for s in range(4):
            base = c * SLAB + 16 + s * ROWS
            pieces = []
            for f in (1, 2, 3):
                for o in (0, 8, 16, -16, -8):
                    piece = sums[f][base + o : base + o + ROWS]
                    if f == 1 and o == 16:
                        piece = jnp.where(last, north(sums[0][base + 8 : base + 16]), piece)
                    if f == 1 and o == -16:
                        piece = jnp.where(head, south(sums[0][base - 8 : base]), piece)
                    pieces.append(piece)
            pieces.append(sums[0][base : base + ROWS])
            message[c * 4 + s] = jnp.concatenate(pieces, axis=0).astype(BF)


def first_step(quarter, tracer, mixing, own, opposite, partner, base, reply, factors, halo, mix_halo, work):
    mine = quarter[0]
    before, after = edge_sides(mine, partner)
    _, wet_before, wet_after, _ = (strip[24:32] for strip in strips(mine, opposite, partner))
    halo[...] = jnp.zeros_like(halo)
    mix_halo[...] = jnp.zeros_like(mix_halo)
    halo[pl.ds(0, LEVELS, stride=ROWS), :] = after[0:32]
    halo[pl.ds(1, LEVELS, stride=ROWS), :] = after[32:64]
    halo[pl.ds(6, LEVELS, stride=ROWS), :] = before[0:32]
    halo[pl.ds(7, LEVELS, stride=ROWS), :] = before[32:64]
    mix_halo[pl.ds(0, LEVELS, stride=ROWS), :] = after[64:96]
    mix_halo[pl.ds(7, LEVELS, stride=ROWS), :] = before[64:96]
    lower = lax.broadcasted_iota(jnp.int32, (ROWS, LANES), 0) < 4
    wet = jnp.concatenate(
        [own[24:32], jnp.where(lower, wet_after, wet_before)], axis=0
    )
    face_e = wet * east(wet)
    face_n = wet * north(wet)
    face_w = west(face_e)
    face_s = south(face_n)

    def level(ref, own, l):
        return jnp.concatenate([own[l], ref[l * ROWS : (l + 1) * ROWS, :]], axis=0)

    zero = jnp.zeros((2 * ROWS, LANES), F32)
    over, ratio, solved, gone = zero, zero, zero, zero
    for l in range(LEVELS):
        t = level(halo, tracer, l)
        explicit = t + spread_gain * (
            face_e * (east(t) - t)
            - face_w * (t - west(t))
            + face_n * (north(t) - t)
            - face_s * (t - south(t))
        )
        under = level(mix_halo, mixing, l) if l < LEVELS - 1 else zero
        inverse = 1.0 / (1.0 + under + over * (1.0 - ratio))
        carry = over * inverse
        ratio = under * inverse
        solved = explicit * inverse + carry * solved
        gone = carry * gone if l else inverse
        factors[0, l] = inverse[0:ROWS]
        factors[1, l] = carry[0:ROWS]
        factors[2, l] = ratio[0:ROWS]
        work[l] = ratio
        base[l] = solved
        reply[l] = gone
        over = under
    for l in range(LEVELS - 2, -1, -1):
        solved = base[l] + work[l] * solved
        gone = reply[l] + work[l] * gone
        base[l] = solved
        reply[l] = gone


def ocean(
    quarter, flux, own, opposite, partner, base, reply, factors,
    tracer_out, height_out, message, work,
):
    mine = quarter[0]
    before2, before, after, after2 = strips(mine, opposite, partner)

    def ring(i, own):
        r = slice(i * ROWS, (i + 1) * ROWS)
        return jnp.concatenate([own, after[r], after2[r], before2[r], before[r]], axis=0)

    total = flux[0].astype(F32)
    for p in range(1, GROUP):
        total = total + flux[p].astype(F32)
    wet = ring(3, own[24:32])
    rain = fresh_gain * total[0:40] * wet
    push_e = stress_gain * total[40:80]
    push_n = stress_gain * total[80:120]
    h = ring(0, own[0:8])
    flow_e = ring(1, own[8:16])
    flow_n = ring(2, own[16:24])
    face_e = wet * east(wet)
    face_n = wet * north(wet)
    face_w, flow_w, push_w = west(face_e), west(flow_e), west(push_e)
    face_s, flow_s, push_s = south(face_n), south(flow_n), south(push_n)
    for _ in range(NSTEP * NSUB):
        flow_e = face_e * (flow_e - wave_gain * (east(h) - h) + push_e)
        flow_w = face_w * (flow_w - wave_gain * (h - west(h)) + push_w)
        flow_n = face_n * (flow_n - wave_gain * (north(h) - h) + push_n)
        flow_s = face_s * (flow_s - wave_gain * (h - south(h)) + push_s)
        h = h - wave_gain * (flow_e - flow_w + flow_n - flow_s) + rain
    height_out[...] = h[0:ROWS]

    wet16 = jnp.concatenate([wet[0:ROWS], jnp.where(
        lax.broadcasted_iota(jnp.int32, (ROWS, LANES), 0) < 4, wet[8:16], wet[32:40])], axis=0)
    tile = lax.broadcasted_iota(jnp.int32, (ROWS, LANES), 0)
    after_heat = jnp.where(tile == 0, south(total[16:24]), 0.0)
    before_heat = jnp.where(tile == ROWS - 1, north(total[24:32]), 0.0)
    heat = jnp.concatenate([total[120:128], after_heat + before_heat], axis=0)
    warm = heating_gain * heat * wet16
    fe, fw, fn, fs = face_e[0:ROWS], face_w[0:ROWS], face_n[0:ROWS], face_s[0:ROWS]
    solved = None
    for l in range(LEVELS):
        both = base[l] + reply[l] * warm
        t = both[0:ROWS]
        explicit = t + spread_gain * (
            fe * (east(t) - t)
            - fw * (t - west(t))
            + fn * (north(both)[0:ROWS] - t)
            - fs * (t - south(both)[0:ROWS])
        )
        if l == 0:
            explicit = explicit + warm[0:ROWS]
            solved = explicit * factors[0, l]
        else:
            solved = explicit * factors[0, l] + factors[1, l] * solved
        work[l] = solved
    tracer_out[LEVELS - 1] = solved
    for l in range(LEVELS - 2, -1, -1):
        solved = work[l] + factors[2, l] * solved
        tracer_out[l] = solved
    top = jnp.concatenate([solved, h[0:ROWS]], axis=0).astype(BF)
    for p in range(GROUP):
        message[p] = top


def answer(place, rows_named, received, message):
    spot = place[0]
    have = received[...].reshape(GROUP * 16, LANES)
    lines = lax.broadcasted_iota(jnp.int32, (GROUP * 16, LANES), 0)
    line_row = (lines >> 6) * 512 + spot * 32 + ((lines >> 4) & 3) * ROWS + (lines & 7)
    second = (lines & 8) != 0
    for q in range(4):
        named = rows_named[q : q + 1, :].astype(jnp.int32)
        same = line_row == named
        for f in range(2):
            picks = jnp.where(same & (second == bool(f)), 1.0, 0.0).astype(BF)
            out = lax.dot_general(
                picks, have, (((0,), (0,)), ((), ())), preferred_element_type=F32
            ).astype(BF)
            message[4 * q : 4 * q + 4, f * 32 : f * 32 + 32, :] = out.reshape(4, 32, LANES)


def finish(received, weights, tracer, height, out, tracer_out, height_out, flat, done):
    saves = [
        pltpu.make_async_copy(tracer, tracer_out, done.at[0]),
        pltpu.make_async_copy(height, height_out, done.at[1]),
    ]
    for save in saves:
        save.start()
    total = received[0].astype(F32)
    for p in range(1, GROUP):
        total = total + received[p].astype(F32)
    flat[...] = total
    for s in range(0, 8, 2):
        answer = None
        for k in (0, 2):
            left = jnp.concatenate(
                [
                    jnp.concatenate(
                        [flat[pl.ds(i * 4 + j, 2, stride=TERMS), :] for j in (k, k + 1)], axis=1
                    )
                    for i in (s, s + 1)
                ],
                axis=0,
            ).astype(BF)
            right = jnp.concatenate(
                [
                    jnp.concatenate([weights[i, k], weights[i, k + 1]], axis=1)
                    for i in (s, s + 1)
                ],
                axis=0,
            )
            part = lax.dot_general(
                left, right, (((1,), (1,)), ((), ())), preferred_element_type=F32
            )
            answer = part if answer is None else answer + part
        out[:, s * LANES : (s + 1) * LANES] = answer[0:2, 0:LANES].astype(BF)
        out[:, (s + 1) * LANES : (s + 2) * LANES] = answer[2:4, LANES:].astype(BF)
    for save in saves:
        save.wait()


def shards(airside, matrices, latitude, tracer, mixing, height, flow, marine):
    spot = lax.axis_index(PLANE).astype(jnp.int32)
    turn = lax.axis_index(("h", "k")).astype(jnp.int32)
    place, quarter = spot.reshape(1), turn.reshape(1)
    count = lax.axis_size(ALL)

    leaving, both, own, weights, first = call(
        prepare,
        (
            inside((128, LANES), BF),
            inside((2, 96, LANES), BF),
            inside((32, LANES), F32),
            inside((8, 4, LANES, LANES), BF),
            shaped((GROUP, 144, LANES), BF),
        ),
        [smem, smem] + [far] * 8,
        [
            pltpu.VMEM((LEVELS, ROWS, LANES), F32),
            pltpu.VMEM((LEVELS - 1, ROWS, LANES), F32),
            pltpu.VMEM((ROWS, LANES), jnp.int32),
            pltpu.VMEM((4, 8), jnp.int32),
            pltpu.VMEM((4, 8 * LANES), BF),
            pltpu.VMEM((4 * TERMS, LANES), F32),
            pltpu.VMEM((144, LANES), BF),
            pltpu.SemaphoreType.DMA((16,)),
        ],
        out_specs=(vmem, vmem, vmem, vmem, far),
        room=60 * 1024,
    )(
        place, quarter, tracer, mixing, height, flow, marine,
        latitude[0].T, airside[0], matrices[0],
    )
    leaving, both, own, weights = map(near, (leaving, both, own, weights))
    pairs = []
    for i in range(count):
        j = i + 4 if i & 2 else i - 4
        if 0 <= j < count:
            pairs.append((i, j))
    arrived = near(lax.ppermute(leaving, ALL, pairs))
    first = near(lax.all_to_all(first, PLANE, 0, 0, tiled=True))

    opposite = call(
        quad_edges, inside((160, LANES), BF), [smem] + [vmem] * 3
    )(quarter, leaving, both, arrived)
    leaving_quad = opposite
    opposite = near(lax.ppermute(leaving_quad, ALL, [(i, i ^ 2) for i in range(count)]))

    second, rows_named = call(
        sort_terms,
        (inside((GROUP, 128, LANES), BF), inside((ROWS, LANES), F32)),
        [smem, vmem, vmem],
    )(place, first, near(leaving_quad))
    rows_named = near(rows_named)
    second = near(lax.all_to_all(second, LINE, 0, 0, tiled=True))

    partner = call(
        pair_edges, inside((288, LANES), BF), [smem] + [vmem] * 4
    )(quarter, leaving, both, opposite, rows_named)
    partner = near(lax.ppermute(partner, ALL, [(i, i ^ 1) for i in range(count)]))

    base, reply, factors = call(
        first_step,
        (
            inside((LEVELS, 2 * ROWS, LANES), F32),
            inside((LEVELS, 2 * ROWS, LANES), F32),
            inside((3, LEVELS, ROWS, LANES), F32),
        ),
        [smem] + [vmem] * 5,
        [
            pltpu.VMEM((LEVELS * ROWS, LANES), F32),
            pltpu.VMEM((LEVELS * ROWS, LANES), F32),
            pltpu.VMEM((LEVELS, 2 * ROWS, LANES), F32),
        ],
    )(quarter, tracer, mixing, own, opposite, partner)

    tracer_new, height_new, third = call(
        ocean,
        (
            inside((LEVELS, ROWS, LANES), F32),
            inside((ROWS, LANES), F32),
            inside((GROUP, 16, LANES), BF),
        ),
        [smem] + [vmem] * 7,
        [pltpu.VMEM((LEVELS, ROWS, LANES), F32)],
    )(quarter, second, own, opposite, partner, near(base), near(reply), near(factors))
    third = near(lax.all_to_all(third, LINE, 0, 0, tiled=True))

    fourth = call(
        answer, inside((GROUP, 64, LANES), BF), [smem, vmem, vmem]
    )(place, rows_named, third)
    fourth = near(lax.all_to_all(fourth, PLANE, 0, 0, tiled=True))

    returned, tracer_new, height_new = call(
        finish,
        (
            shaped((2, 8 * LANES), BF),
            shaped((LEVELS, ROWS, LANES), F32),
            shaped((ROWS, LANES), F32),
        ),
        [vmem] * 4,
        [pltpu.VMEM((2 * TERMS, LANES), F32), pltpu.SemaphoreType.DMA((2,))],
        out_specs=(vmem, far, far),
    )(fourth, weights, near(tracer_new), near(height_new))
    return tracer_new, height_new, returned[None]


def solution(mesh):
    split = Mesh(mesh.devices.reshape(4, 4, 4, 2, 2), ALL)
    dom = ("y", "x", "h", "k")
    return jax.shard_map(
        shards,
        mesh=split,
        in_specs=(
            P("c", None, dom),
            P("c", dom, None, None, None),
            P("c", dom, None),
            P(None, ALL, None),
            P(None, ALL, None),
            P(ALL, None),
            P(None, ALL, None),
            P(ALL, None),
        ),
        out_specs=(P(None, ALL, None), P(ALL, None), P("c", None, dom)),
        check_vma=False,
    )
```

```python
import jax
import jax.numpy as jnp
from jax import lax
from jax.experimental import pallas as pl
from jax.experimental.pallas import tpu as pltpu
from jax.sharding import Mesh, PartitionSpec as P

NSTEP = 2
NSUB = 8

wave_gain = 0.35
stress_gain = 0.1
fresh_gain = 0.1
spread_gain = 0.2
heating_gain = 0.5

ALL = ("c", "y", "x", "h", "k")
PLANE = ("y", "x")
LINE = ("c", "h", "k")
ROWS = 8
LANES = 128
LEVELS = 32
TERMS = 32
GROUP = 16
SLAB = 64
BF = jnp.bfloat16
F32 = jnp.float32

vmem = pl.BlockSpec(memory_space=pltpu.VMEM)
smem = pl.BlockSpec(memory_space=pltpu.SMEM)
far = pl.BlockSpec(memory_space=pltpu.HBM)


def call(kernel, outs, ins, scratch=(), out_specs=None, room=12 << 10):
    return pl.pallas_call(
        kernel,
        out_shape=outs,
        in_specs=ins,
        out_specs=jax.tree.map(lambda _: vmem, outs) if out_specs is None else out_specs,
        scratch_shapes=list(scratch),
        compiler_params=pltpu.CompilerParams(vmem_limit_bytes=room << 10),
    )


def shaped(shape, kind):
    return jax.ShapeDtypeStruct(shape, kind)


def inside(shape, kind):
    return pltpu.VMEM(shape, kind)


def near(value):
    return pltpu.with_memory_space_constraint(value, pltpu.VMEM)


def east(v):
    return pltpu.roll(v, LANES - 1, axis=v.ndim - 1)


def west(v):
    return pltpu.roll(v, 1, axis=v.ndim - 1)


def north(v):
    return pltpu.roll(v, v.shape[0] - 1, axis=0)


def south(v):
    return pltpu.roll(v, 1, axis=0)


def prepare(
    place, quarter, tracer_far, mixing_far, height_far, flow_far, wet_far, targets_far, sources_far,
    weights_far, leaving, both, own, weights, message,
    tracer, mixing, wet, targets, sources, flat, packet, done,
):
    def load(source, target, i):
        copy = pltpu.make_async_copy(source, target, done.at[i])
        copy.start()
        return copy

    edges = [
        load(tracer_far, tracer, 0),
        load(mixing_far, mixing, 1),
        load(height_far, own.at[0:8], 2),
        load(flow_far.at[0], own.at[8:16], 3),
        load(flow_far.at[1], own.at[16:24], 4),
        load(wet_far, wet, 5),
    ]
    small = [load(targets_far, targets, 6), load(sources_far, sources, 7)]
    large = [load(weights_far.at[s], weights.at[s], 8 + s) for s in range(8)]
    for copy in edges:
        copy.wait()
    own[24:32] = wet[...].astype(F32)
    zero = jnp.zeros((1, LANES), F32)
    for i, (first, second, rim) in enumerate(((6, 7, 7), (0, 1, 0))):
        both[i, 0:32] = tracer[:, first, :].astype(BF)
        both[i, 32:64] = tracer[:, second, :].astype(BF)
        both[i, 64:96] = jnp.concatenate([mixing[:, rim, :], zero], axis=0).astype(BF)
    leaving[0:32] = own[...].astype(BF)
    leaving[32:128] = both[1 - (quarter[0] & 1)]
    for copy in small:
        copy.wait()
    lane = lax.broadcasted_iota(jnp.int32, (4, LANES), 1)
    link = lax.broadcasted_iota(jnp.int32, (4, LANES), 0)
    mine = (lane >> 5 == (place[0] & 3)) & ((lane & 3) == link)
    named = jnp.zeros((4, LANES), jnp.int32)
    for s in range(8):
        column = jnp.broadcast_to(targets[:, s : s + 1], (4, LANES))
        named = named + jnp.where(mine & ((lane & 31) >> 2 == s), column, 0)
    named = jnp.broadcast_to(jnp.sum(named, axis=0, keepdims=True), (ROWS, LANES))
    line = lax.broadcasted_iota(jnp.int32, (ROWS, LANES), 0)
    coded = jnp.where(line == 0, named >> 6, jnp.where(line == 1, named & 63, 0)).astype(F32)
    coded = jnp.concatenate([coded, jnp.zeros((ROWS, LANES), F32)], axis=0).astype(BF)
    packet[128:144] = coded
    blank = jnp.zeros((4, LANES), F32)
    for s in range(0, 8, 2):
        some = [sources[:, i * LANES : (i + 1) * LANES].astype(F32) for i in (s, s + 1)]
        left = jnp.concatenate(
            [
                jnp.concatenate([some[0], blank], axis=1),
                jnp.concatenate([blank, some[1]], axis=1),
            ],
            axis=0,
        ).astype(BF)
        large[s].wait()
        large[s + 1].wait()
        for k in (0, 2):
            right = jnp.concatenate(
                [
                    jnp.concatenate([weights[i, k], weights[i, k + 1]], axis=1)
                    for i in (s, s + 1)
                ],
                axis=0,
            )
            out = jnp.dot(left, right, preferred_element_type=F32)
            for i in range(2):
                for j in range(2):
                    flat[pl.ds((s + i) * 4 + k + j, 4, stride=TERMS), :] = out[
                        4 * i : 4 * i + 4, j * LANES : (j + 1) * LANES
                    ]
    packet[0:128] = flat[...].astype(BF)
    sent = [load(packet, message.at[p], p) for p in range(GROUP)]
    for copy in sent:
        copy.wait()


def pair_edges(quarter, leaving, both, opposite, outer, _after, message):
    mine = quarter[0]
    message[0:32] = leaving[0:32]
    message[32:64] = opposite[0:32]
    message[64:96] = outer[0:32]
    message[96:192] = both[mine & 1]
    ends = (mine == 0) | (mine == 3)

    @pl.when(ends)
    def _():
        message[192:288] = opposite[32:128]

    @pl.when(jnp.logical_not(ends))
    def _():
        message[192:288] = outer[32:128]


def edge_sides(mine, partner):
    first = (mine & 1) == 0
    near_edge = partner[96:192].astype(F32)
    far_edge = partner[192:288].astype(F32)
    return jnp.where(first, far_edge, near_edge), jnp.where(first, near_edge, far_edge)


def strips(mine, opposite, outer, partner):
    first = (mine & 1) == 0
    low = mine < 2
    beside = partner[0:32].astype(F32)
    ours = (opposite[0:32].astype(F32), outer[0:32].astype(F32))
    theirs = (partner[32:64].astype(F32), partner[64:96].astype(F32))
    prev_own = jnp.where(low, ours[1], ours[0])
    prev_other = jnp.where(low, theirs[1], theirs[0])
    next_own = jnp.where(low, ours[0], ours[1])
    next_other = jnp.where(low, theirs[0], theirs[1])
    before2 = prev_own
    before = jnp.where(first, prev_other, beside)
    after = jnp.where(first, beside, next_other)
    after2 = next_own
    return before2, before, after, after2


def sort_terms(place, received, message, rows_named):
    spot = place[0]
    lines = lax.broadcasted_iota(jnp.int32, (4 * SLAB, LANES), 0)
    line_row = (lines >> 6) * 512 + spot * 32 - 16 + (lines & (SLAB - 1))
    sums = [None] * 4
    tile = lax.broadcasted_iota(jnp.int32, (ROWS, LANES), 0)
    head, last = tile == 0, tile == ROWS - 1
    for q in range(4):
        coded = sum(received[4 * q + i, 128:144, :].astype(F32) for i in range(4))
        named = coded[0:1] * 64.0 + coded[1:2]
        rows_named[q : q + 1, :] = named
        picks = jnp.where(line_row == named.astype(jnp.int32), 1.0, 0.0).astype(BF)
        for f in range(4):
            some = received[4 * q : 4 * q + 4, f * 32 : f * 32 + 32, :].reshape(LANES, LANES)
            part = jnp.dot(picks, some, preferred_element_type=F32)
            sums[f] = part if sums[f] is None else sums[f] + part
    for c in range(4):
        for h in range(2):
            base = c * SLAB + 16 + h * 16
            heat, rain, push_e, push_n = (
                sums[f][base - 16 : base + 32] for f in range(4)
            )
            pieces = [
                jnp.where(head, south(heat[8:16]), rain[0:8]),
                rain[8:40],
                jnp.where(last, north(heat[32:40]), rain[40:48]),
                push_e,
                push_n,
                heat[16:32],
            ]
            message[c * 2 + h] = jnp.concatenate(pieces, axis=0).astype(BF)


def add_up(received, total):
    some = received[0].astype(F32)
    for p in range(1, 8):
        some = some + received[p].astype(F32)
    total[...] = some


def first_step(quarter, tracer, mixing, own, opposite, outer, partner, base, reply, factors, halo, mix_halo, work):
    mine = quarter[0]
    before, after = edge_sides(mine, partner)
    _, wet_before, wet_after, _ = (strip[24:32] for strip in strips(mine, opposite, outer, partner))
    halo[...] = jnp.zeros_like(halo)
    mix_halo[...] = jnp.zeros_like(mix_halo)
    halo[pl.ds(0, LEVELS, stride=ROWS), :] = after[0:32]
    halo[pl.ds(1, LEVELS, stride=ROWS), :] = after[32:64]
    halo[pl.ds(6, LEVELS, stride=ROWS), :] = before[0:32]
    halo[pl.ds(7, LEVELS, stride=ROWS), :] = before[32:64]
    mix_halo[pl.ds(0, LEVELS, stride=ROWS), :] = after[64:96]
    mix_halo[pl.ds(7, LEVELS, stride=ROWS), :] = before[64:96]
    lower = lax.broadcasted_iota(jnp.int32, (ROWS, LANES), 0) < 4
    wet = jnp.concatenate(
        [own[24:32], jnp.where(lower, wet_after, wet_before)], axis=0
    )
    face_e = wet * east(wet)
    face_n = wet * north(wet)
    face_w = west(face_e)
    face_s = south(face_n)

    def level(ref, own, l):
        return jnp.concatenate([own[l], ref[l * ROWS : (l + 1) * ROWS, :]], axis=0)

    zero = jnp.zeros((2 * ROWS, LANES), F32)
    over, ratio, solved, gone = zero, zero, zero, zero
    for l in range(LEVELS):
        t = level(halo, tracer, l)
        explicit = t + spread_gain * (
            face_e * (east(t) - t)
            - face_w * (t - west(t))
            + face_n * (north(t) - t)
            - face_s * (t - south(t))
        )
        under = level(mix_halo, mixing, l) if l < LEVELS - 1 else zero
        inverse = 1.0 / (1.0 + under + over * (1.0 - ratio))
        carry = over * inverse
        ratio = under * inverse
        solved = explicit * inverse + carry * solved
        gone = carry * gone if l else inverse
        factors[0, l] = inverse[0:ROWS]
        factors[1, l] = carry[0:ROWS]
        factors[2, l] = ratio[0:ROWS]
        work[l] = ratio
        base[l] = solved
        reply[l] = gone
        over = under
    for l in range(LEVELS - 2, -1, -1):
        solved = base[l] + work[l] * solved
        gone = reply[l] + work[l] * gone
        base[l] = solved
        reply[l] = gone


def ocean(
    quarter, flux, flux_beside, own, opposite, outer, partner, base, reply, factors,
    tracer_out, height_out, message, work,
):
    mine = quarter[0]
    before2, before, after, after2 = strips(mine, opposite, outer, partner)

    def ring(i, own):
        r = slice(i * ROWS, (i + 1) * ROWS)
        return jnp.concatenate([own, after[r], after2[r], before2[r], before[r]], axis=0)

    first = (mine & 1) == 0
    total = flux[...] + flux_beside[...]

    def window(start):
        blocks = [total[start + i * ROWS : start + (i + 1) * ROWS] for i in range(6)]
        parts = [jnp.where(first, blocks[i], blocks[i + 1]) for i in (2, 3, 4, 0, 1)]
        return jnp.concatenate(parts, axis=0)

    wet = ring(3, own[24:32])
    rain = fresh_gain * window(0) * wet
    push_e = stress_gain * window(48)
    push_n = stress_gain * window(96)
    h = ring(0, own[0:8])
    flow_e = ring(1, own[8:16])
    flow_n = ring(2, own[16:24])
    face_e = wet * east(wet)
    face_n = wet * north(wet)
    face_w, flow_w, push_w = west(face_e), west(flow_e), west(push_e)
    face_s, flow_s, push_s = south(face_n), south(flow_n), south(push_n)
    for _ in range(NSTEP * NSUB):
        flow_e = face_e * (flow_e - wave_gain * (east(h) - h) + push_e)
        flow_w = face_w * (flow_w - wave_gain * (h - west(h)) + push_w)
        flow_n = face_n * (flow_n - wave_gain * (north(h) - h) + push_n)
        flow_s = face_s * (flow_s - wave_gain * (h - south(h)) + push_s)
        h = h - wave_gain * (flow_e - flow_w + flow_n - flow_s) + rain
    height_out[...] = h[0:ROWS]

    wet16 = jnp.concatenate([wet[0:ROWS], jnp.where(
        lax.broadcasted_iota(jnp.int32, (ROWS, LANES), 0) < 4, wet[8:16], wet[32:40])], axis=0)
    tile = lax.broadcasted_iota(jnp.int32, (ROWS, LANES), 0)
    heat_low, heat_high = total[144:152], total[152:160]
    after_heat = jnp.where(first, heat_high, south(total[40:48]))
    before_heat = jnp.where(first, north(total[0:8]), heat_low)
    halo_heat = jnp.where(tile == 0, after_heat, jnp.where(tile == ROWS - 1, before_heat, 0.0))
    heat = jnp.concatenate([jnp.where(first, heat_low, heat_high), halo_heat], axis=0)
    warm = heating_gain * heat * wet16
    fe, fw, fn, fs = face_e[0:ROWS], face_w[0:ROWS], face_n[0:ROWS], face_s[0:ROWS]
    solved = None
    for l in range(LEVELS):
        both = base[l] + reply[l] * warm
        t = both[0:ROWS]
        explicit = t + spread_gain * (
            fe * (east(t) - t)
            - fw * (t - west(t))
            + fn * (north(both)[0:ROWS] - t)
            - fs * (t - south(both)[0:ROWS])
        )
        if l == 0:
            explicit = explicit + warm[0:ROWS]
            solved = explicit * factors[0, l]
        else:
            solved = explicit * factors[0, l] + factors[1, l] * solved
        work[l] = solved
    tracer_out[LEVELS - 1] = solved
    for l in range(LEVELS - 2, -1, -1):
        solved = work[l] + factors[2, l] * solved
        tracer_out[l] = solved
    top = jnp.concatenate([solved, h[0:ROWS]], axis=0).astype(BF)
    for p in range(GROUP):
        message[p] = top


def answer(place, rows_named, received, message):
    spot = place[0]
    have = received[...].reshape(GROUP * 16, LANES)
    lines = lax.broadcasted_iota(jnp.int32, (GROUP * 16, LANES), 0)
    line_row = (lines >> 6) * 512 + spot * 32 + ((lines >> 4) & 3) * ROWS + (lines & 7)
    second = (lines & 8) != 0
    for q in range(4):
        named = rows_named[q : q + 1, :].astype(jnp.int32)
        same = line_row == named
        for f in range(2):
            picks = jnp.where(same & (second == bool(f)), 1.0, 0.0).astype(BF)
            out = lax.dot_general(
                picks, have, (((0,), (0,)), ((), ())), preferred_element_type=F32
            ).astype(BF)
            message[4 * q : 4 * q + 4, f * 32 : f * 32 + 32, :] = out.reshape(4, 32, LANES)


def finish(received, weights, tracer, height, out, tracer_out, height_out, flat, done):
    saves = [
        pltpu.make_async_copy(tracer, tracer_out, done.at[0]),
        pltpu.make_async_copy(height, height_out, done.at[1]),
    ]
    for save in saves:
        save.start()
    total = received[0].astype(F32)
    for p in range(1, GROUP):
        total = total + received[p].astype(F32)
    flat[...] = total
    for s in range(0, 8, 2):
        answer = None
        for k in (0, 2):
            left = jnp.concatenate(
                [
                    jnp.concatenate(
                        [flat[pl.ds(i * 4 + j, 2, stride=TERMS), :] for j in (k, k + 1)], axis=1
                    )
                    for i in (s, s + 1)
                ],
                axis=0,
            ).astype(BF)
            right = jnp.concatenate(
                [
                    jnp.concatenate([weights[i, k], weights[i, k + 1]], axis=1)
                    for i in (s, s + 1)
                ],
                axis=0,
            )
            part = lax.dot_general(
                left, right, (((1,), (1,)), ((), ())), preferred_element_type=F32
            )
            answer = part if answer is None else answer + part
        out[:, s * LANES : (s + 1) * LANES] = answer[0:2, 0:LANES].astype(BF)
        out[:, (s + 1) * LANES : (s + 2) * LANES] = answer[2:4, LANES:].astype(BF)
    for save in saves:
        save.wait()


def shards(airside, matrices, latitude, tracer, mixing, height, flow, marine):
    spot = lax.axis_index(PLANE).astype(jnp.int32)
    turn = lax.axis_index(("h", "k")).astype(jnp.int32)
    place, quarter = spot.reshape(1), turn.reshape(1)
    count = lax.axis_size(ALL)

    leaving, both, own, weights, first = call(
        prepare,
        (
            inside((128, LANES), BF),
            inside((2, 96, LANES), BF),
            inside((32, LANES), F32),
            inside((8, 4, LANES, LANES), BF),
            shaped((GROUP, 144, LANES), BF),
        ),
        [smem, smem] + [far] * 8,
        [
            pltpu.VMEM((LEVELS, ROWS, LANES), F32),
            pltpu.VMEM((LEVELS - 1, ROWS, LANES), F32),
            pltpu.VMEM((ROWS, LANES), jnp.int32),
            pltpu.VMEM((4, 8), jnp.int32),
            pltpu.VMEM((4, 8 * LANES), BF),
            pltpu.VMEM((4 * TERMS, LANES), F32),
            pltpu.VMEM((144, LANES), BF),
            pltpu.SemaphoreType.DMA((16,)),
        ],
        out_specs=(vmem, vmem, vmem, vmem, far),
        room=60 * 1024,
    )(
        place, quarter, tracer, mixing, height, flow, marine,
        latitude[0].T, airside[0], matrices[0],
    )
    leaving, both, own, weights = map(near, (leaving, both, own, weights))
    first = near(lax.all_to_all(first, PLANE, 0, 0, tiled=True))
    opposite = near(lax.ppermute(leaving, ALL, [(i, i ^ 2) for i in range(count)]))
    pairs = []
    for i in range(count):
        j = i + 2 if i & 2 else i - 2
        if 0 <= j < count:
            pairs.append((i, j))
    outer = near(lax.ppermute(leaving, ALL, pairs))

    second, rows_named = call(
        sort_terms, (inside((8, 160, LANES), BF), inside((ROWS, LANES), F32)), [smem, vmem]
    )(place, first)
    rows_named = near(rows_named)
    second = near(lax.all_to_all(second, ("c", "h"), 0, 0, tiled=True))
    flux = near(call(add_up, inside((160, LANES), F32), [vmem])(second))
    flux_beside = near(lax.ppermute(flux, ALL, [(i, i ^ 1) for i in range(count)]))

    partner = call(
        pair_edges, inside((288, LANES), BF), [smem] + [vmem] * 5
    )(quarter, leaving, both, opposite, outer, rows_named)
    partner = near(lax.ppermute(partner, ALL, [(i, i ^ 1) for i in range(count)]))

    base, reply, factors = call(
        first_step,
        (
            inside((LEVELS, 2 * ROWS, LANES), F32),
            inside((LEVELS, 2 * ROWS, LANES), F32),
            inside((3, LEVELS, ROWS, LANES), F32),
        ),
        [smem] + [vmem] * 6,
        [
            pltpu.VMEM((LEVELS * ROWS, LANES), F32),
            pltpu.VMEM((LEVELS * ROWS, LANES), F32),
            pltpu.VMEM((LEVELS, 2 * ROWS, LANES), F32),
        ],
    )(quarter, tracer, mixing, own, opposite, outer, partner)

    tracer_new, height_new, third = call(
        ocean,
        (
            inside((LEVELS, ROWS, LANES), F32),
            inside((ROWS, LANES), F32),
            inside((GROUP, 16, LANES), BF),
        ),
        [smem] + [vmem] * 9,
        [pltpu.VMEM((LEVELS, ROWS, LANES), F32)],
    )(quarter, flux, flux_beside, own, opposite, outer, partner, near(base), near(reply), near(factors))
    third = near(lax.all_to_all(third, LINE, 0, 0, tiled=True))

    fourth = call(
        answer, inside((GROUP, 64, LANES), BF), [smem, vmem, vmem]
    )(place, rows_named, third)
    fourth = near(lax.all_to_all(fourth, PLANE, 0, 0, tiled=True))

    returned, tracer_new, height_new = call(
        finish,
        (
            shaped((2, 8 * LANES), BF),
            shaped((LEVELS, ROWS, LANES), F32),
            shaped((ROWS, LANES), F32),
        ),
        [vmem] * 4,
        [pltpu.VMEM((2 * TERMS, LANES), F32), pltpu.SemaphoreType.DMA((2,))],
        out_specs=(vmem, far, far),
    )(fourth, weights, near(tracer_new), near(height_new))
    return tracer_new, height_new, returned[None]


def solution(mesh):
    split = Mesh(mesh.devices.reshape(4, 4, 4, 2, 2), ALL)
    dom = ("y", "x", "h", "k")
    return jax.shard_map(
        shards,
        mesh=split,
        in_specs=(
            P("c", None, dom),
            P("c", dom, None, None, None),
            P("c", dom, None),
            P(None, ALL, None),
            P(None, ALL, None),
            P(ALL, None),
            P(None, ALL, None),
            P(ALL, None),
        ),
        out_specs=(P(None, ALL, None), P(ALL, None), P("c", None, dom)),
        check_vma=False,
    )
```

```python
import jax
import jax.numpy as jnp
from jax import lax
from jax.experimental import pallas as pl
from jax.experimental.pallas import tpu as pltpu
from jax.sharding import Mesh, PartitionSpec as P

NSTEP = 2
NSUB = 8

wave_gain = 0.35
stress_gain = 0.1
fresh_gain = 0.1
spread_gain = 0.2
heating_gain = 0.5

ALL = ("c", "y", "x", "h", "k")
PLANE = ("y", "x")
LINE = ("c", "h", "k")
ROWS = 8
LANES = 128
LEVELS = 32
TERMS = 32
GROUP = 16
SLAB = 64
BF = jnp.bfloat16
F32 = jnp.float32

vmem = pl.BlockSpec(memory_space=pltpu.VMEM)
smem = pl.BlockSpec(memory_space=pltpu.SMEM)
far = pl.BlockSpec(memory_space=pltpu.HBM)


def call(kernel, outs, ins, scratch=(), out_specs=None, room=12 << 10):
    return pl.pallas_call(
        kernel,
        out_shape=outs,
        in_specs=ins,
        out_specs=jax.tree.map(lambda _: vmem, outs) if out_specs is None else out_specs,
        scratch_shapes=list(scratch),
        compiler_params=pltpu.CompilerParams(vmem_limit_bytes=room << 10),
    )


def shaped(shape, kind):
    return jax.ShapeDtypeStruct(shape, kind)


def inside(shape, kind):
    return pltpu.VMEM(shape, kind)


def near(value):
    return pltpu.with_memory_space_constraint(value, pltpu.VMEM)


def east(v):
    return pltpu.roll(v, LANES - 1, axis=v.ndim - 1)


def west(v):
    return pltpu.roll(v, 1, axis=v.ndim - 1)


def north(v):
    return pltpu.roll(v, v.shape[0] - 1, axis=0)


def south(v):
    return pltpu.roll(v, 1, axis=0)


def prepare(
    place, tracer_far, mixing_far, height_far, flow_far, wet_far, targets_far, sources_far,
    weights_far, leaving, own, weights, message,
    tracer, mixing, wet, targets, sources, flat, packet, done, sent,
):
    def load(source, target, flag):
        copy = pltpu.make_async_copy(source, target, flag)
        copy.start()
        return copy

    small = [load(targets_far, targets, done.at[6]), load(sources_far, sources, done.at[7])]
    large = [load(weights_far.at[s], weights.at[s], done.at[8 + s]) for s in range(8)]
    edges = [
        load(tracer_far, tracer, done.at[0]),
        load(mixing_far, mixing, done.at[1]),
        load(height_far, own.at[0:8], done.at[2]),
        load(flow_far.at[0], own.at[8:16], done.at[3]),
        load(flow_far.at[1], own.at[16:24], done.at[4]),
        load(wet_far, wet, done.at[5]),
    ]
    for copy in small:
        copy.wait()
    lane = lax.broadcasted_iota(jnp.int32, (4, LANES), 1)
    link = lax.broadcasted_iota(jnp.int32, (4, LANES), 0)
    mine = (lane >> 5 == (place[0] & 3)) & ((lane & 3) == link)
    named = jnp.zeros((4, LANES), jnp.int32)
    for s in range(8):
        column = jnp.broadcast_to(targets[:, s : s + 1], (4, LANES))
        named = named + jnp.where(mine & ((lane & 31) >> 2 == s), column, 0)
    named = jnp.broadcast_to(jnp.sum(named, axis=0, keepdims=True), (ROWS, LANES))
    line = lax.broadcasted_iota(jnp.int32, (ROWS, LANES), 0)
    coded = jnp.where(line == 0, named >> 6, jnp.where(line == 1, named & 63, 0)).astype(F32)
    coded = jnp.concatenate([coded, jnp.zeros((ROWS, LANES), F32)], axis=0).astype(BF)
    packet[128:144] = coded
    blank = jnp.zeros((4, LANES), F32)
    for s in range(0, 8, 2):
        some = [sources[:, i * LANES : (i + 1) * LANES].astype(F32) for i in (s, s + 1)]
        left = jnp.concatenate(
            [
                jnp.concatenate([some[0], blank], axis=1),
                jnp.concatenate([blank, some[1]], axis=1),
            ],
            axis=0,
        ).astype(BF)
        large[s].wait()
        large[s + 1].wait()
        for k in (0, 2):
            right = jnp.concatenate(
                [
                    jnp.concatenate([weights[i, k], weights[i, k + 1]], axis=1)
                    for i in (s, s + 1)
                ],
                axis=0,
            )
            out = jnp.dot(left, right, preferred_element_type=F32)
            for i in range(2):
                for j in range(2):
                    flat[pl.ds((s + i) * 4 + k + j, 4, stride=TERMS), :] = out[
                        4 * i : 4 * i + 4, j * LANES : (j + 1) * LANES
                    ]
    packet[0:128] = flat[...].astype(BF)
    copies = [load(packet, message.at[p], sent.at[p]) for p in range(GROUP)]
    for copy in edges:
        copy.wait()
    own[24:32] = wet[...].astype(F32)
    zero = jnp.zeros((1, LANES), F32)
    for i, (first, second, rim) in enumerate(((6, 7, 7), (0, 1, 0))):
        at = 32 + 96 * i
        leaving[at : at + 32] = tracer[:, first, :].astype(BF)
        leaving[at + 32 : at + 64] = tracer[:, second, :].astype(BF)
        leaving[at + 64 : at + 96] = jnp.concatenate(
            [mixing[:, rim, :], zero], axis=0
        ).astype(BF)
    leaving[0:32] = own[...].astype(BF)
    for copy in copies:
        copy.wait()


def chip_edges(quarter, leaving, beside, message):
    mine = quarter[0]
    core = mine & 1
    own = pl.multiple_of(32 * core, 32)
    other = pl.multiple_of(32 - 32 * core, 32)
    message[pl.ds(own, 32)] = leaving[0:32]
    message[pl.ds(other, 32)] = beside[0:32]
    for i, (source, start) in enumerate(
        ((beside, 32), (beside, 128), (leaving, 128), (leaving, 32))
    ):

        @pl.when(mine == i)
        def _(source=source, start=start):
            message[64:160] = source[start : start + 96]


def edge_sides(mine, beside, mixed, shared):
    first = (mine & 1) == 0
    near_edge = jnp.where(first, beside[128:224].astype(F32), beside[32:128].astype(F32))
    far_edge = jnp.where(mine < 2, shared[64:160].astype(F32), mixed[64:160].astype(F32))
    return jnp.where(first, far_edge, near_edge), jnp.where(first, near_edge, far_edge)


def strips(mine, beside, mixed, shared):
    first = (mine & 1) == 0
    low = mine < 2
    ours, theirs = mixed[0:64].astype(F32), shared[0:64].astype(F32)
    swap = first == low
    prev = jnp.where(swap, theirs, ours)
    follow = jnp.where(swap, ours, theirs)
    partner = beside[0:32].astype(F32)
    before2 = jnp.where(first, prev[0:32], prev[32:64])
    before = jnp.where(first, prev[32:64], partner)
    after = jnp.where(first, partner, follow[0:32])
    after2 = jnp.where(first, follow[0:32], follow[32:64])
    return before2, before, after, after2


def sort_terms(place, received, message, rows_named):
    spot = place[0]
    lines = lax.broadcasted_iota(jnp.int32, (4 * SLAB, LANES), 0)
    line_row = (lines >> 6) * 512 + spot * 32 - 16 + (lines & (SLAB - 1))
    sums = [None] * 4
    tile = lax.broadcasted_iota(jnp.int32, (ROWS, LANES), 0)
    head, last = tile == 0, tile == ROWS - 1
    for q in range(4):
        coded = sum(received[4 * q + i, 128:144, :].astype(F32) for i in range(4))
        named = coded[0:1] * 64.0 + coded[1:2]
        rows_named[q : q + 1, :] = named
        picks = jnp.where(line_row == named.astype(jnp.int32), 1.0, 0.0).astype(BF)
        for f in range(4):
            some = received[4 * q : 4 * q + 4, f * 32 : f * 32 + 32, :].reshape(LANES, LANES)
            part = jnp.dot(picks, some, preferred_element_type=F32)
            sums[f] = part if sums[f] is None else sums[f] + part
    for c in range(4):
        for h in range(2):
            base = c * SLAB + 16 + h * 16
            heat, rain, push_e, push_n = (
                sums[f][base - 16 : base + 32] for f in range(4)
            )
            pieces = [
                jnp.where(head, south(heat[8:16]), rain[0:8]),
                rain[8:40],
                jnp.where(last, north(heat[32:40]), rain[40:48]),
                push_e,
                push_n,
                heat[16:32],
            ]
            message[c * 2 + h] = jnp.concatenate(pieces, axis=0).astype(BF)


def add_up(received, total):
    some = received[0].astype(F32)
    for p in range(1, 8):
        some = some + received[p].astype(F32)
    total[...] = some


def first_step(quarter, tracer, mixing, own, beside, mixed, shared, base, reply, factors, halo, mix_halo, work):
    mine = quarter[0]
    before, after = edge_sides(mine, beside, mixed, shared)
    _, wet_before, wet_after, _ = (strip[24:32] for strip in strips(mine, beside, mixed, shared))
    halo[...] = jnp.zeros_like(halo)
    mix_halo[...] = jnp.zeros_like(mix_halo)
    halo[pl.ds(0, LEVELS, stride=ROWS), :] = after[0:32]
    halo[pl.ds(1, LEVELS, stride=ROWS), :] = after[32:64]
    halo[pl.ds(6, LEVELS, stride=ROWS), :] = before[0:32]
    halo[pl.ds(7, LEVELS, stride=ROWS), :] = before[32:64]
    mix_halo[pl.ds(0, LEVELS, stride=ROWS), :] = after[64:96]
    mix_halo[pl.ds(7, LEVELS, stride=ROWS), :] = before[64:96]
    lower = lax.broadcasted_iota(jnp.int32, (ROWS, LANES), 0) < 4
    wet = jnp.concatenate(
        [own[24:32], jnp.where(lower, wet_after, wet_before)], axis=0
    )
    face_e = wet * east(wet)
    face_n = wet * north(wet)
    face_w = west(face_e)
    face_s = south(face_n)

    def level(ref, own, l):
        return jnp.concatenate([own[l], ref[l * ROWS : (l + 1) * ROWS, :]], axis=0)

    zero = jnp.zeros((2 * ROWS, LANES), F32)
    over, ratio, solved, gone = zero, zero, zero, zero
    for l in range(LEVELS):
        t = level(halo, tracer, l)
        explicit = t + spread_gain * (
            face_e * (east(t) - t)
            - face_w * (t - west(t))
            + face_n * (north(t) - t)
            - face_s * (t - south(t))
        )
        under = level(mix_halo, mixing, l) if l < LEVELS - 1 else zero
        inverse = 1.0 / (1.0 + under + over * (1.0 - ratio))
        carry = over * inverse
        ratio = under * inverse
        solved = explicit * inverse + carry * solved
        gone = carry * gone if l else inverse
        factors[0, l] = inverse[0:ROWS]
        factors[1, l] = carry[0:ROWS]
        factors[2, l] = ratio[0:ROWS]
        work[l] = ratio
        base[l] = solved
        reply[l] = gone
        over = under
    for l in range(LEVELS - 2, -1, -1):
        solved = base[l] + work[l] * solved
        gone = reply[l] + work[l] * gone
        base[l] = solved
        reply[l] = gone


def ocean(
    quarter, flux, flux_beside, own, beside, mixed, shared, base, reply, factors,
    tracer_out, height_out, message, work,
):
    mine = quarter[0]
    before2, before, after, after2 = strips(mine, beside, mixed, shared)

    def ring(i, own):
        r = slice(i * ROWS, (i + 1) * ROWS)
        return jnp.concatenate([own, after[r], after2[r], before2[r], before[r]], axis=0)

    first = (mine & 1) == 0
    total = flux[...] + flux_beside[...]

    def window(start):
        blocks = [total[start + i * ROWS : start + (i + 1) * ROWS] for i in range(6)]
        parts = [jnp.where(first, blocks[i], blocks[i + 1]) for i in (2, 3, 4, 0, 1)]
        return jnp.concatenate(parts, axis=0)

    wet = ring(3, own[24:32])
    rain = fresh_gain * window(0) * wet
    push_e = stress_gain * window(48)
    push_n = stress_gain * window(96)
    h = ring(0, own[0:8])
    flow_e = ring(1, own[8:16])
    flow_n = ring(2, own[16:24])
    face_e = wet * east(wet)
    face_n = wet * north(wet)
    face_w, flow_w, push_w = west(face_e), west(flow_e), west(push_e)
    face_s, flow_s, push_s = south(face_n), south(flow_n), south(push_n)
    for turn in range(NSTEP * NSUB):
        if turn == NSUB:

            def inner(v):
                return jnp.concatenate([v[0:16], v[32:40]], axis=0)

            h, flow_e, flow_w, flow_n, flow_s = map(inner, (h, flow_e, flow_w, flow_n, flow_s))
            face_e, face_w, face_n, face_s = map(inner, (face_e, face_w, face_n, face_s))
            push_e, push_w, push_n, push_s = map(inner, (push_e, push_w, push_n, push_s))
            rain = inner(rain)
        flow_e = face_e * (flow_e - wave_gain * (east(h) - h) + push_e)
        flow_w = face_w * (flow_w - wave_gain * (h - west(h)) + push_w)
        flow_n = face_n * (flow_n - wave_gain * (north(h) - h) + push_n)
        flow_s = face_s * (flow_s - wave_gain * (h - south(h)) + push_s)
        h = h - wave_gain * (flow_e - flow_w + flow_n - flow_s) + rain
    height_out[...] = h[0:ROWS]

    wet16 = jnp.concatenate([wet[0:ROWS], jnp.where(
        lax.broadcasted_iota(jnp.int32, (ROWS, LANES), 0) < 4, wet[8:16], wet[32:40])], axis=0)
    tile = lax.broadcasted_iota(jnp.int32, (ROWS, LANES), 0)
    heat_low, heat_high = total[144:152], total[152:160]
    after_heat = jnp.where(first, heat_high, south(total[40:48]))
    before_heat = jnp.where(first, north(total[0:8]), heat_low)
    halo_heat = jnp.where(tile == 0, after_heat, jnp.where(tile == ROWS - 1, before_heat, 0.0))
    heat = jnp.concatenate([jnp.where(first, heat_low, heat_high), halo_heat], axis=0)
    warm = heating_gain * heat * wet16
    fe, fw, fn, fs = face_e[0:ROWS], face_w[0:ROWS], face_n[0:ROWS], face_s[0:ROWS]
    solved = None
    for l in range(LEVELS):
        both = base[l] + reply[l] * warm
        t = both[0:ROWS]
        explicit = t + spread_gain * (
            fe * (east(t) - t)
            - fw * (t - west(t))
            + fn * (north(both)[0:ROWS] - t)
            - fs * (t - south(both)[0:ROWS])
        )
        if l == 0:
            explicit = explicit + warm[0:ROWS]
            solved = explicit * factors[0, l]
        else:
            solved = explicit * factors[0, l] + factors[1, l] * solved
        work[l] = solved
    tracer_out[LEVELS - 1] = solved
    for l in range(LEVELS - 2, -1, -1):
        solved = work[l] + factors[2, l] * solved
        tracer_out[l] = solved
    top = jnp.concatenate([solved, h[0:ROWS]], axis=0).astype(BF)
    for p in range(GROUP):
        message[p] = top


def answer(place, rows_named, received, message):
    spot = place[0]
    have = received[...].reshape(GROUP * 16, LANES)
    lines = lax.broadcasted_iota(jnp.int32, (GROUP * 16, LANES), 0)
    line_row = (lines >> 6) * 512 + spot * 32 + ((lines >> 4) & 3) * ROWS + (lines & 7)
    second = (lines & 8) != 0
    for q in range(4):
        named = rows_named[q : q + 1, :].astype(jnp.int32)
        same = line_row == named
        for f in range(2):
            picks = jnp.where(same & (second == bool(f)), 1.0, 0.0).astype(BF)
            out = lax.dot_general(
                picks, have, (((0,), (0,)), ((), ())), preferred_element_type=F32
            ).astype(BF)
            message[4 * q : 4 * q + 4, f * 32 : f * 32 + 32, :] = out.reshape(4, 32, LANES)


def finish(received, weights, tracer, height, out_far, tracer_out, height_out, flat, out, done):
    saves = [
        pltpu.make_async_copy(tracer, tracer_out, done.at[0]),
        pltpu.make_async_copy(height, height_out, done.at[1]),
    ]
    for save in saves:
        save.start()
    total = received[0].astype(F32)
    for p in range(1, GROUP):
        total = total + received[p].astype(F32)
    flat[...] = total
    for s in range(0, 8, 2):
        answer = None
        for k in (0, 2):
            left = jnp.concatenate(
                [
                    jnp.concatenate(
                        [flat[pl.ds(i * 4 + j, 2, stride=TERMS), :] for j in (k, k + 1)], axis=1
                    )
                    for i in (s, s + 1)
                ],
                axis=0,
            ).astype(BF)
            right = jnp.concatenate(
                [
                    jnp.concatenate([weights[i, k], weights[i, k + 1]], axis=1)
                    for i in (s, s + 1)
                ],
                axis=0,
            )
            part = lax.dot_general(
                left, right, (((1,), (1,)), ((), ())), preferred_element_type=F32
            )
            answer = part if answer is None else answer + part
        out[:, s * LANES : (s + 1) * LANES] = answer[0:2, 0:LANES].astype(BF)
        out[:, (s + 1) * LANES : (s + 2) * LANES] = answer[2:4, LANES:].astype(BF)
    last = pltpu.make_async_copy(out, out_far, done.at[2])
    last.start()
    for save in (*saves, last):
        save.wait()


def shards(airside, matrices, latitude, tracer, mixing, height, flow, marine):
    spot = lax.axis_index(PLANE).astype(jnp.int32)
    turn = lax.axis_index(("h", "k")).astype(jnp.int32)
    place, quarter = spot.reshape(1), turn.reshape(1)
    count = lax.axis_size(ALL)

    leaving, own, weights, first = call(
        prepare,
        (
            inside((224, LANES), BF),
            inside((32, LANES), F32),
            inside((8, 4, LANES, LANES), BF),
            shaped((GROUP, 144, LANES), BF),
        ),
        [smem] + [far] * 8,
        [
            pltpu.VMEM((LEVELS, ROWS, LANES), F32),
            pltpu.VMEM((LEVELS - 1, ROWS, LANES), F32),
            pltpu.VMEM((ROWS, LANES), jnp.int32),
            pltpu.VMEM((4, 8), jnp.int32),
            pltpu.VMEM((4, 8 * LANES), BF),
            pltpu.VMEM((4 * TERMS, LANES), F32),
            pltpu.VMEM((144, LANES), BF),
            pltpu.SemaphoreType.DMA((16,)),
            pltpu.SemaphoreType.DMA((16,)),
        ],
        out_specs=(vmem, vmem, vmem, far),
        room=60 * 1024,
    )(
        place, tracer, mixing, height, flow, marine,
        latitude[0].T, airside[0], matrices[0],
    )
    leaving, own, weights = map(near, (leaving, own, weights))
    first = near(lax.all_to_all(first, PLANE, 0, 0, tiled=True))
    flip = [(i, i ^ 1) for i in range(count)]
    pairs = []
    for i in range(count):
        up = bool(i & 2) == bool(i & 1)
        j = i + 2 if up else i - 2
        if 0 <= j < count:
            pairs.append((i, j))
    beside = near(lax.ppermute(leaving, ALL, flip))
    mixed = call(
        chip_edges, inside((160, LANES), BF), [smem] + [vmem] * 2
    )(quarter, leaving, beside)
    mixed = near(lax.ppermute(near(mixed), ALL, pairs))

    second, rows_named = call(
        sort_terms, (inside((8, 160, LANES), BF), inside((ROWS, LANES), F32)), [smem, vmem]
    )(place, first)
    rows_named = near(rows_named)
    second = near(lax.all_to_all(second, ("c", "h"), 0, 0, tiled=True))
    flux = near(call(add_up, inside((160, LANES), F32), [vmem])(second))
    flux_beside = near(lax.ppermute(flux, ALL, flip))

    shared = near(lax.ppermute(mixed, ALL, flip))

    base, reply, factors = call(
        first_step,
        (
            inside((LEVELS, 2 * ROWS, LANES), F32),
            inside((LEVELS, 2 * ROWS, LANES), F32),
            inside((3, LEVELS, ROWS, LANES), F32),
        ),
        [smem] + [vmem] * 6,
        [
            pltpu.VMEM((LEVELS * ROWS, LANES), F32),
            pltpu.VMEM((LEVELS * ROWS, LANES), F32),
            pltpu.VMEM((LEVELS, 2 * ROWS, LANES), F32),
        ],
    )(quarter, tracer, mixing, own, beside, mixed, shared)

    tracer_new, height_new, third = call(
        ocean,
        (
            inside((LEVELS, ROWS, LANES), F32),
            inside((ROWS, LANES), F32),
            inside((GROUP, 16, LANES), BF),
        ),
        [smem] + [vmem] * 9,
        [pltpu.VMEM((LEVELS, ROWS, LANES), F32)],
    )(quarter, flux, flux_beside, own, beside, mixed, shared, near(base), near(reply), near(factors))
    third = near(lax.all_to_all(third, LINE, 0, 0, tiled=True))

    fourth = call(
        answer, inside((GROUP, 64, LANES), BF), [smem, vmem, vmem]
    )(place, rows_named, third)
    fourth = near(lax.all_to_all(fourth, PLANE, 0, 0, tiled=True))

    returned, tracer_new, height_new = call(
        finish,
        (
            shaped((2, 8 * LANES), BF),
            shaped((LEVELS, ROWS, LANES), F32),
            shaped((ROWS, LANES), F32),
        ),
        [vmem] * 4,
        [
            pltpu.VMEM((2 * TERMS, LANES), F32),
            pltpu.VMEM((2, 8 * LANES), BF),
            pltpu.SemaphoreType.DMA((3,)),
        ],
        out_specs=(far, far, far),
    )(fourth, weights, near(tracer_new), near(height_new))
    return tracer_new, height_new, returned[None]


def solution(mesh):
    split = Mesh(mesh.devices.reshape(4, 4, 4, 2, 2), ALL)
    dom = ("y", "x", "h", "k")
    return jax.shard_map(
        shards,
        mesh=split,
        in_specs=(
            P("c", None, dom),
            P("c", dom, None, None, None),
            P("c", dom, None),
            P(None, ALL, None),
            P(None, ALL, None),
            P(ALL, None),
            P(None, ALL, None),
            P(ALL, None),
        ),
        out_specs=(P(None, ALL, None), P(ALL, None), P("c", None, dom)),
        check_vma=False,
    )
```

```python
import jax
import jax.numpy as jnp
from jax import lax
from jax.experimental import pallas as pl
from jax.experimental.pallas import tpu as pltpu
from jax.sharding import Mesh, PartitionSpec as P

NSTEP = 2
NSUB = 8

wave_gain = 0.35
stress_gain = 0.1
fresh_gain = 0.1
spread_gain = 0.2
heating_gain = 0.5

ALL = ("c", "y", "x", "h", "k")
PLANE = ("y", "x")
LINE = ("c", "h", "k")
ROWS = 8
LANES = 128
LEVELS = 32
TERMS = 32
GROUP = 16
SLAB = 64
BF = jnp.bfloat16
F32 = jnp.float32

vmem = pl.BlockSpec(memory_space=pltpu.VMEM)
smem = pl.BlockSpec(memory_space=pltpu.SMEM)
far = pl.BlockSpec(memory_space=pltpu.HBM)


def call(kernel, outs, ins, scratch=(), out_specs=None, room=12 << 10):
    return pl.pallas_call(
        kernel,
        out_shape=outs,
        in_specs=ins,
        out_specs=jax.tree.map(lambda _: vmem, outs) if out_specs is None else out_specs,
        scratch_shapes=list(scratch),
        compiler_params=pltpu.CompilerParams(vmem_limit_bytes=room << 10),
    )


def shaped(shape, kind):
    return jax.ShapeDtypeStruct(shape, kind)


def inside(shape, kind):
    return pltpu.VMEM(shape, kind)


def near(value):
    return pltpu.with_memory_space_constraint(value, pltpu.VMEM)


def east(v):
    return pltpu.roll(v, LANES - 1, axis=v.ndim - 1)


def west(v):
    return pltpu.roll(v, 1, axis=v.ndim - 1)


def north(v):
    return pltpu.roll(v, v.shape[0] - 1, axis=0)


def south(v):
    return pltpu.roll(v, 1, axis=0)


def prepare(
    place, tracer_far, mixing_far, height_far, flow_far, wet_far, targets_far, sources_far,
    weights_far, leaving, own, weights, tracer, mixing, message,
    wet, targets, sources, flat, packet, done, sent,
):
    def load(source, target, flag):
        copy = pltpu.make_async_copy(source, target, flag)
        copy.start()
        return copy

    small = [load(targets_far, targets, done.at[6]), load(sources_far, sources, done.at[7])]
    large = [load(weights_far.at[s], weights.at[s], done.at[8 + s]) for s in range(8)]
    edges = [
        load(tracer_far, tracer, done.at[0]),
        load(mixing_far, mixing, done.at[1]),
        load(height_far, own.at[0:8], done.at[2]),
        load(flow_far.at[0], own.at[8:16], done.at[3]),
        load(flow_far.at[1], own.at[16:24], done.at[4]),
        load(wet_far, wet, done.at[5]),
    ]
    for copy in small:
        copy.wait()
    lane = lax.broadcasted_iota(jnp.int32, (4, LANES), 1)
    link = lax.broadcasted_iota(jnp.int32, (4, LANES), 0)
    mine = (lane >> 5 == (place[0] & 3)) & ((lane & 3) == link)
    named = jnp.zeros((4, LANES), jnp.int32)
    for s in range(8):
        column = jnp.broadcast_to(targets[:, s : s + 1], (4, LANES))
        named = named + jnp.where(mine & ((lane & 31) >> 2 == s), column, 0)
    named = jnp.broadcast_to(jnp.sum(named, axis=0, keepdims=True), (ROWS, LANES))
    line = lax.broadcasted_iota(jnp.int32, (ROWS, LANES), 0)
    coded = jnp.where(line == 0, named >> 6, jnp.where(line == 1, named & 63, 0)).astype(F32)
    coded = jnp.concatenate([coded, jnp.zeros((ROWS, LANES), F32)], axis=0).astype(BF)
    packet[128:144] = coded
    blank = jnp.zeros((4, LANES), F32)
    for s in range(0, 8, 2):
        some = [sources[:, i * LANES : (i + 1) * LANES].astype(F32) for i in (s, s + 1)]
        left = jnp.concatenate(
            [
                jnp.concatenate([some[0], blank], axis=1),
                jnp.concatenate([blank, some[1]], axis=1),
            ],
            axis=0,
        ).astype(BF)
        large[s].wait()
        large[s + 1].wait()
        for k in (0, 2):
            right = jnp.concatenate(
                [
                    jnp.concatenate([weights[i, k], weights[i, k + 1]], axis=1)
                    for i in (s, s + 1)
                ],
                axis=0,
            )
            out = jnp.dot(left, right, preferred_element_type=F32)
            for i in range(2):
                for j in range(2):
                    flat[pl.ds((s + i) * 4 + k + j, 4, stride=TERMS), :] = out[
                        4 * i : 4 * i + 4, j * LANES : (j + 1) * LANES
                    ]
    packet[0:128] = flat[...].astype(BF)
    copies = [load(packet, message.at[p], sent.at[p]) for p in range(GROUP)]
    for copy in edges:
        copy.wait()
    own[24:32] = wet[...].astype(F32)
    zero = jnp.zeros((1, LANES), F32)
    for i, (first, second, rim) in enumerate(((6, 7, 7), (0, 1, 0))):
        at = 32 + 96 * i
        leaving[at : at + 32] = tracer[:, first, :].astype(BF)
        leaving[at + 32 : at + 64] = tracer[:, second, :].astype(BF)
        leaving[at + 64 : at + 96] = jnp.concatenate(
            [mixing[:, rim, :], zero], axis=0
        ).astype(BF)
    leaving[0:32] = own[...].astype(BF)
    for copy in copies:
        copy.wait()


def chip_edges(quarter, leaving, beside, message):
    mine = quarter[0]
    core = mine & 1
    own = pl.multiple_of(32 * core, 32)
    other = pl.multiple_of(32 - 32 * core, 32)
    message[pl.ds(own, 32)] = leaving[0:32]
    message[pl.ds(other, 32)] = beside[0:32]
    for i, (source, start) in enumerate(
        ((beside, 32), (beside, 128), (leaving, 128), (leaving, 32))
    ):

        @pl.when(mine == i)
        def _(source=source, start=start):
            message[64:160] = source[start : start + 96]


def edge_sides(mine, beside, mixed, shared):
    first = (mine & 1) == 0
    near_edge = jnp.where(first, beside[128:224].astype(F32), beside[32:128].astype(F32))
    far_edge = jnp.where(mine < 2, shared[64:160].astype(F32), mixed[64:160].astype(F32))
    return jnp.where(first, far_edge, near_edge), jnp.where(first, near_edge, far_edge)


def strips(mine, beside, mixed, shared):
    first = (mine & 1) == 0
    low = mine < 2
    ours, theirs = mixed[0:64].astype(F32), shared[0:64].astype(F32)
    swap = first == low
    prev = jnp.where(swap, theirs, ours)
    follow = jnp.where(swap, ours, theirs)
    partner = beside[0:32].astype(F32)
    before2 = jnp.where(first, prev[0:32], prev[32:64])
    before = jnp.where(first, prev[32:64], partner)
    after = jnp.where(first, partner, follow[0:32])
    after2 = jnp.where(first, follow[0:32], follow[32:64])
    return before2, before, after, after2


def sort_terms(place, received, message, rows_named):
    spot = place[0]
    lines = lax.broadcasted_iota(jnp.int32, (4 * SLAB, LANES), 0)
    line_row = (lines >> 6) * 512 + spot * 32 - 16 + (lines & (SLAB - 1))
    sums = [None] * 4
    tile = lax.broadcasted_iota(jnp.int32, (ROWS, LANES), 0)
    head, last = tile == 0, tile == ROWS - 1
    for q in range(4):
        coded = sum(received[4 * q + i, 128:144, :].astype(F32) for i in range(4))
        named = coded[0:1] * 64.0 + coded[1:2]
        rows_named[q : q + 1, :] = named
        picks = jnp.where(line_row == named.astype(jnp.int32), 1.0, 0.0).astype(BF)
        for f in range(4):
            some = received[4 * q : 4 * q + 4, f * 32 : f * 32 + 32, :].reshape(LANES, LANES)
            part = jnp.dot(picks, some, preferred_element_type=F32)
            sums[f] = part if sums[f] is None else sums[f] + part
    for c in range(4):
        for h in range(2):
            base = c * SLAB + 16 + h * 16
            heat, rain, push_e, push_n = (
                sums[f][base - 16 : base + 32] for f in range(4)
            )
            pieces = [
                jnp.where(head, south(heat[8:16]), rain[0:8]),
                rain[8:40],
                jnp.where(last, north(heat[32:40]), rain[40:48]),
                push_e,
                push_n,
                heat[16:32],
            ]
            message[c * 2 + h] = jnp.concatenate(pieces, axis=0).astype(BF)


def add_up(received, total):
    some = received[0].astype(F32)
    for p in range(1, 8):
        some = some + received[p].astype(F32)
    total[...] = some


def first_step(quarter, tracer, mixing, own, beside, mixed, shared, base, reply, factors, halo, mix_halo, work):
    mine = quarter[0]
    before, after = edge_sides(mine, beside, mixed, shared)
    _, wet_before, wet_after, _ = (strip[24:32] for strip in strips(mine, beside, mixed, shared))
    halo[...] = jnp.zeros_like(halo)
    mix_halo[...] = jnp.zeros_like(mix_halo)
    halo[pl.ds(0, LEVELS, stride=ROWS), :] = after[0:32]
    halo[pl.ds(1, LEVELS, stride=ROWS), :] = after[32:64]
    halo[pl.ds(6, LEVELS, stride=ROWS), :] = before[0:32]
    halo[pl.ds(7, LEVELS, stride=ROWS), :] = before[32:64]
    mix_halo[pl.ds(0, LEVELS, stride=ROWS), :] = after[64:96]
    mix_halo[pl.ds(7, LEVELS, stride=ROWS), :] = before[64:96]
    lower = lax.broadcasted_iota(jnp.int32, (ROWS, LANES), 0) < 4
    wet = jnp.concatenate(
        [own[24:32], jnp.where(lower, wet_after, wet_before)], axis=0
    )
    face_e = wet * east(wet)
    face_n = wet * north(wet)
    face_w = west(face_e)
    face_s = south(face_n)

    def level(ref, own, l):
        return jnp.concatenate([own[l], ref[l * ROWS : (l + 1) * ROWS, :]], axis=0)

    zero = jnp.zeros((2 * ROWS, LANES), F32)
    over, ratio, solved, gone = zero, zero, zero, zero
    for l in range(LEVELS):
        t = level(halo, tracer, l)
        explicit = t + spread_gain * (
            face_e * (east(t) - t)
            - face_w * (t - west(t))
            + face_n * (north(t) - t)
            - face_s * (t - south(t))
        )
        under = level(mix_halo, mixing, l) if l < LEVELS - 1 else zero
        inverse = 1.0 / (1.0 + under + over * (1.0 - ratio))
        carry = over * inverse
        ratio = under * inverse
        solved = explicit * inverse + carry * solved
        gone = carry * gone if l else inverse
        factors[0, l] = inverse[0:ROWS]
        factors[1, l] = carry[0:ROWS]
        factors[2, l] = ratio[0:ROWS]
        work[l] = ratio
        base[l] = solved
        reply[l] = gone
        over = under
    for l in range(LEVELS - 2, -1, -1):
        solved = base[l] + work[l] * solved
        gone = reply[l] + work[l] * gone
        base[l] = solved
        reply[l] = gone


def ocean(
    quarter, flux, flux_beside, own, beside, mixed, shared, base, reply, factors,
    tracer_out, height_out, message, work,
):
    mine = quarter[0]
    before2, before, after, after2 = strips(mine, beside, mixed, shared)

    def ring(i, own):
        r = slice(i * ROWS, (i + 1) * ROWS)
        return jnp.concatenate([own, after[r], after2[r], before2[r], before[r]], axis=0)

    first = (mine & 1) == 0
    total = flux[...] + flux_beside[...]

    def window(start):
        blocks = [total[start + i * ROWS : start + (i + 1) * ROWS] for i in range(6)]
        parts = [jnp.where(first, blocks[i], blocks[i + 1]) for i in (2, 3, 4, 0, 1)]
        return jnp.concatenate(parts, axis=0)

    wet = ring(3, own[24:32])
    rain = fresh_gain * window(0) * wet
    h = ring(0, own[0:8])
    face_e = wet * east(wet)
    face_n = wet * north(wet)
    flow_e = wave_gain * ring(1, own[8:16])
    flow_n = wave_gain * ring(2, own[16:24])
    push_e = (wave_gain * stress_gain) * window(48)
    push_n = (wave_gain * stress_gain) * window(96)
    face_w, flow_w, push_w = west(face_e), west(flow_e), west(push_e)
    face_s, flow_s, push_s = south(face_n), south(flow_n), south(push_n)
    slope = wave_gain * wave_gain
    slope_e, slope_w, slope_n, slope_s = (
        slope * face for face in (face_e, face_w, face_n, face_s)
    )
    for turn in range(NSTEP * NSUB):
        if turn == NSUB:

            def inner(v):
                return jnp.concatenate([v[0:16], v[32:40]], axis=0)

            h, flow_e, flow_w, flow_n, flow_s = map(inner, (h, flow_e, flow_w, flow_n, flow_s))
            face_e, face_w, face_n, face_s = map(inner, (face_e, face_w, face_n, face_s))
            push_e, push_w, push_n, push_s = map(inner, (push_e, push_w, push_n, push_s))
            slope_e, slope_w, slope_n, slope_s = map(inner, (slope_e, slope_w, slope_n, slope_s))
            rain = inner(rain)
        flow_e = face_e * (flow_e + push_e) - slope_e * (east(h) - h)
        flow_w = face_w * (flow_w + push_w) - slope_w * (h - west(h))
        flow_n = face_n * (flow_n + push_n) - slope_n * (north(h) - h)
        flow_s = face_s * (flow_s + push_s) - slope_s * (h - south(h))
        h = (h + rain) - ((flow_e - flow_w) + (flow_n - flow_s))
    height_out[...] = h[0:ROWS]

    wet16 = jnp.concatenate([wet[0:ROWS], jnp.where(
        lax.broadcasted_iota(jnp.int32, (ROWS, LANES), 0) < 4, wet[8:16], wet[32:40])], axis=0)
    tile = lax.broadcasted_iota(jnp.int32, (ROWS, LANES), 0)
    heat_low, heat_high = total[144:152], total[152:160]
    after_heat = jnp.where(first, heat_high, south(total[40:48]))
    before_heat = jnp.where(first, north(total[0:8]), heat_low)
    halo_heat = jnp.where(tile == 0, after_heat, jnp.where(tile == ROWS - 1, before_heat, 0.0))
    heat = jnp.concatenate([jnp.where(first, heat_low, heat_high), halo_heat], axis=0)
    warm = heating_gain * heat * wet16
    fe, fw, fn, fs = face_e[0:ROWS], face_w[0:ROWS], face_n[0:ROWS], face_s[0:ROWS]
    solved = None
    for l in range(LEVELS):
        both = base[l] + reply[l] * warm
        t = both[0:ROWS]
        explicit = t + spread_gain * (
            fe * (east(t) - t)
            - fw * (t - west(t))
            + fn * (north(both)[0:ROWS] - t)
            - fs * (t - south(both)[0:ROWS])
        )
        if l == 0:
            explicit = explicit + warm[0:ROWS]
            solved = explicit * factors[0, l]
        else:
            solved = explicit * factors[0, l] + factors[1, l] * solved
        work[l] = solved
    tracer_out[LEVELS - 1] = solved
    for l in range(LEVELS - 2, -1, -1):
        solved = work[l] + factors[2, l] * solved
        tracer_out[l] = solved
    top = jnp.concatenate([solved, h[0:ROWS]], axis=0).astype(BF)
    for p in range(GROUP):
        message[p] = top


def answer(place, rows_named, received, message):
    spot = place[0]
    have = received[...].reshape(GROUP * 16, LANES)
    lines = lax.broadcasted_iota(jnp.int32, (GROUP * 16, LANES), 0)
    line_row = (lines >> 6) * 512 + spot * 32 + ((lines >> 4) & 3) * ROWS + (lines & 7)
    second = (lines & 8) != 0
    for q in range(4):
        named = rows_named[q : q + 1, :].astype(jnp.int32)
        same = line_row == named
        for f in range(2):
            picks = jnp.where(same & (second == bool(f)), 1.0, 0.0).astype(BF)
            out = lax.dot_general(
                picks, have, (((0,), (0,)), ((), ())), preferred_element_type=F32
            ).astype(BF)
            message[4 * q : 4 * q + 4, f * 32 : f * 32 + 32, :] = out.reshape(4, 32, LANES)


def finish(received, weights, tracer, height, out_far, tracer_out, height_out, flat, out, done):
    saves = [
        pltpu.make_async_copy(tracer, tracer_out, done.at[0]),
        pltpu.make_async_copy(height, height_out, done.at[1]),
    ]
    for save in saves:
        save.start()
    total = received[0].astype(F32)
    for p in range(1, GROUP):
        total = total + received[p].astype(F32)
    flat[...] = total
    for s in range(0, 8, 2):
        answer = None
        for k in (0, 2):
            left = jnp.concatenate(
                [
                    jnp.concatenate(
                        [flat[pl.ds(i * 4 + j, 2, stride=TERMS), :] for j in (k, k + 1)], axis=1
                    )
                    for i in (s, s + 1)
                ],
                axis=0,
            ).astype(BF)
            right = jnp.concatenate(
                [
                    jnp.concatenate([weights[i, k], weights[i, k + 1]], axis=1)
                    for i in (s, s + 1)
                ],
                axis=0,
            )
            part = lax.dot_general(
                left, right, (((1,), (1,)), ((), ())), preferred_element_type=F32
            )
            answer = part if answer is None else answer + part
        out[:, s * LANES : (s + 1) * LANES] = answer[0:2, 0:LANES].astype(BF)
        out[:, (s + 1) * LANES : (s + 2) * LANES] = answer[2:4, LANES:].astype(BF)
    last = pltpu.make_async_copy(out, out_far, done.at[2])
    last.start()
    for save in (*saves, last):
        save.wait()


def shards(airside, matrices, latitude, tracer, mixing, height, flow, marine):
    spot = lax.axis_index(PLANE).astype(jnp.int32)
    turn = lax.axis_index(("h", "k")).astype(jnp.int32)
    place, quarter = spot.reshape(1), turn.reshape(1)
    count = lax.axis_size(ALL)

    leaving, own, weights, tracer, mixing, first = call(
        prepare,
        (
            inside((224, LANES), BF),
            inside((32, LANES), F32),
            inside((8, 4, LANES, LANES), BF),
            inside((LEVELS, ROWS, LANES), F32),
            inside((LEVELS - 1, ROWS, LANES), F32),
            shaped((GROUP, 144, LANES), BF),
        ),
        [smem] + [far] * 8,
        [
            pltpu.VMEM((ROWS, LANES), jnp.int32),
            pltpu.VMEM((4, 8), jnp.int32),
            pltpu.VMEM((4, 8 * LANES), BF),
            pltpu.VMEM((4 * TERMS, LANES), F32),
            pltpu.VMEM((144, LANES), BF),
            pltpu.SemaphoreType.DMA((16,)),
            pltpu.SemaphoreType.DMA((16,)),
        ],
        out_specs=(vmem,) * 5 + (far,),
        room=60 * 1024,
    )(
        place, tracer, mixing, height, flow, marine,
        latitude[0].T, airside[0], matrices[0],
    )
    leaving, own, weights, tracer, mixing = map(near, (leaving, own, weights, tracer, mixing))
    first = near(lax.all_to_all(first, PLANE, 0, 0, tiled=True))
    flip = [(i, i ^ 1) for i in range(count)]
    pairs = []
    for i in range(count):
        up = bool(i & 2) == bool(i & 1)
        j = i + 2 if up else i - 2
        if 0 <= j < count:
            pairs.append((i, j))
    beside = near(lax.ppermute(leaving, ALL, flip))
    mixed = call(
        chip_edges, inside((160, LANES), BF), [smem] + [vmem] * 2
    )(quarter, leaving, beside)
    mixed = near(lax.ppermute(near(mixed), ALL, pairs))

    second, rows_named = call(
        sort_terms, (inside((8, 160, LANES), BF), inside((ROWS, LANES), F32)), [smem, vmem]
    )(place, first)
    rows_named = near(rows_named)
    second = near(lax.all_to_all(second, ("c", "h"), 0, 0, tiled=True))
    flux = near(call(add_up, inside((160, LANES), F32), [vmem])(second))
    flux_beside = near(lax.ppermute(flux, ALL, flip))

    shared = near(lax.ppermute(mixed, ALL, flip))

    base, reply, factors = call(
        first_step,
        (
            inside((LEVELS, 2 * ROWS, LANES), F32),
            inside((LEVELS, 2 * ROWS, LANES), F32),
            inside((3, LEVELS, ROWS, LANES), F32),
        ),
        [smem] + [vmem] * 6,
        [
            pltpu.VMEM((LEVELS * ROWS, LANES), F32),
            pltpu.VMEM((LEVELS * ROWS, LANES), F32),
            pltpu.VMEM((LEVELS, 2 * ROWS, LANES), F32),
        ],
    )(quarter, tracer, mixing, own, beside, mixed, shared)

    tracer_new, height_new, third = call(
        ocean,
        (
            inside((LEVELS, ROWS, LANES), F32),
            inside((ROWS, LANES), F32),
            inside((GROUP, 16, LANES), BF),
        ),
        [smem] + [vmem] * 9,
        [pltpu.VMEM((LEVELS, ROWS, LANES), F32)],
    )(quarter, flux, flux_beside, own, beside, mixed, shared, near(base), near(reply), near(factors))
    third = near(lax.all_to_all(third, LINE, 0, 0, tiled=True))

    fourth = call(
        answer, inside((GROUP, 64, LANES), BF), [smem, vmem, vmem]
    )(place, rows_named, third)
    fourth = near(lax.all_to_all(fourth, PLANE, 0, 0, tiled=True))

    returned, tracer_new, height_new = call(
        finish,
        (
            shaped((2, 8 * LANES), BF),
            shaped((LEVELS, ROWS, LANES), F32),
            shaped((ROWS, LANES), F32),
        ),
        [vmem] * 4,
        [
            pltpu.VMEM((2 * TERMS, LANES), F32),
            pltpu.VMEM((2, 8 * LANES), BF),
            pltpu.SemaphoreType.DMA((3,)),
        ],
        out_specs=(far, far, far),
    )(fourth, weights, near(tracer_new), near(height_new))
    return tracer_new, height_new, returned[None]


def solution(mesh):
    split = Mesh(mesh.devices.reshape(4, 4, 4, 2, 2), ALL)
    dom = ("y", "x", "h", "k")
    return jax.shard_map(
        shards,
        mesh=split,
        in_specs=(
            P("c", None, dom),
            P("c", dom, None, None, None),
            P("c", dom, None),
            P(None, ALL, None),
            P(None, ALL, None),
            P(ALL, None),
            P(None, ALL, None),
            P(ALL, None),
        ),
        out_specs=(P(None, ALL, None), P(ALL, None), P("c", None, dom)),
        check_vma=False,
    )
```

```python
import jax
import jax.numpy as jnp
from jax import lax
from jax.experimental import pallas as pl
from jax.experimental.pallas import tpu as pltpu
from jax.sharding import Mesh, PartitionSpec as P

NSTEP = 2
NSUB = 8

wave_gain = 0.35
stress_gain = 0.1
fresh_gain = 0.1
spread_gain = 0.2
heating_gain = 0.5

ALL = ("c", "y", "x", "h", "k")
PLANE = ("y", "x")
LINE = ("c", "h", "k")
ROWS = 8
LANES = 128
LEVELS = 32
TERMS = 32
GROUP = 16
SLAB = 64
BF = jnp.bfloat16
F32 = jnp.float32

vmem = pl.BlockSpec(memory_space=pltpu.VMEM)
smem = pl.BlockSpec(memory_space=pltpu.SMEM)
far = pl.BlockSpec(memory_space=pltpu.HBM)


def call(kernel, outs, ins, scratch=(), out_specs=None, room=12 << 10):
    return pl.pallas_call(
        kernel,
        out_shape=outs,
        in_specs=ins,
        out_specs=jax.tree.map(lambda _: vmem, outs) if out_specs is None else out_specs,
        scratch_shapes=list(scratch),
        compiler_params=pltpu.CompilerParams(vmem_limit_bytes=room << 10),
    )


def shaped(shape, kind):
    return jax.ShapeDtypeStruct(shape, kind)


def inside(shape, kind):
    return pltpu.VMEM(shape, kind)


def near(value):
    return pltpu.with_memory_space_constraint(value, pltpu.VMEM)


def east(v):
    return pltpu.roll(v, LANES - 1, axis=v.ndim - 1)


def west(v):
    return pltpu.roll(v, 1, axis=v.ndim - 1)


def north(v):
    return pltpu.roll(v, v.shape[0] - 1, axis=0)


def south(v):
    return pltpu.roll(v, 1, axis=0)


def prepare(
    place, tracer_far, mixing_far, height_far, flow_far, wet_far, targets_far, sources_far,
    weights_far, leaving, own, weights, tracer, mixing, message,
    wet, targets, sources, flat, packet, done, sent,
):
    def load(source, target, flag):
        copy = pltpu.make_async_copy(source, target, flag)
        copy.start()
        return copy

    small = [load(targets_far, targets, done.at[6]), load(sources_far, sources, done.at[7])]
    large = [load(weights_far.at[s], weights.at[s], done.at[8 + s]) for s in range(8)]
    edges = [
        load(tracer_far, tracer, done.at[0]),
        load(mixing_far, mixing, done.at[1]),
        load(height_far, own.at[0:8], done.at[2]),
        load(flow_far.at[0], own.at[8:16], done.at[3]),
        load(flow_far.at[1], own.at[16:24], done.at[4]),
        load(wet_far, wet, done.at[5]),
    ]
    for copy in small:
        copy.wait()
    lane = lax.broadcasted_iota(jnp.int32, (4, LANES), 1)
    link = lax.broadcasted_iota(jnp.int32, (4, LANES), 0)
    mine = (lane >> 5 == (place[0] & 3)) & ((lane & 3) == link)
    named = jnp.zeros((4, LANES), jnp.int32)
    for s in range(8):
        column = jnp.broadcast_to(targets[:, s : s + 1], (4, LANES))
        named = named + jnp.where(mine & ((lane & 31) >> 2 == s), column, 0)
    named = jnp.broadcast_to(jnp.sum(named, axis=0, keepdims=True), (ROWS, LANES))
    line = lax.broadcasted_iota(jnp.int32, (ROWS, LANES), 0)
    coded = jnp.where(line == 0, named >> 6, jnp.where(line == 1, named & 63, 0)).astype(F32)
    coded = jnp.concatenate([coded, jnp.zeros((ROWS, LANES), F32)], axis=0).astype(BF)
    packet[128:144] = coded
    blank = jnp.zeros((4, LANES), F32)
    for s in range(0, 8, 2):
        some = [sources[:, i * LANES : (i + 1) * LANES].astype(F32) for i in (s, s + 1)]
        left = jnp.concatenate(
            [
                jnp.concatenate([some[0], blank], axis=1),
                jnp.concatenate([blank, some[1]], axis=1),
            ],
            axis=0,
        ).astype(BF)
        large[s].wait()
        large[s + 1].wait()
        for k in (0, 2):
            right = jnp.concatenate(
                [
                    jnp.concatenate([weights[i, k], weights[i, k + 1]], axis=1)
                    for i in (s, s + 1)
                ],
                axis=0,
            )
            out = jnp.dot(left, right, preferred_element_type=F32)
            for i in range(2):
                for j in range(2):
                    flat[pl.ds((s + i) * 4 + k + j, 4, stride=TERMS), :] = out[
                        4 * i : 4 * i + 4, j * LANES : (j + 1) * LANES
                    ]
    packet[0:128] = flat[...].astype(BF)
    copies = [load(packet, message.at[p], sent.at[p]) for p in range(GROUP)]
    for copy in edges:
        copy.wait()
    own[24:32] = wet[...].astype(F32)
    zero = jnp.zeros((1, LANES), F32)
    for i, (first, second, rim) in enumerate(((6, 7, 7), (0, 1, 0))):
        at = 32 + 96 * i
        leaving[at : at + 32] = tracer[:, first, :].astype(BF)
        leaving[at + 32 : at + 64] = tracer[:, second, :].astype(BF)
        leaving[at + 64 : at + 96] = jnp.concatenate(
            [mixing[:, rim, :], zero], axis=0
        ).astype(BF)
    leaving[0:32] = own[...].astype(BF)
    for copy in copies:
        copy.wait()


def chip_edges(quarter, leaving, beside, across, outward):
    mine = quarter[0]
    core = mine & 1
    own = pl.multiple_of(32 * core, 32)
    other = pl.multiple_of(32 - 32 * core, 32)
    for message in (across, outward):
        message[pl.ds(own, 32)] = leaving[0:32]
        message[pl.ds(other, 32)] = beside[0:32]

    @pl.when(mine < 2)
    def _():
        across[64:160] = beside[32:128]
        outward[64:160] = beside[128:224]

    @pl.when(mine >= 2)
    def _():
        across[64:160] = beside[128:224]
        outward[64:160] = beside[32:128]


def edge_sides(mine, beside, opposite, outer):
    first = (mine & 1) == 0
    ends = (mine == 0) | (mine == 3)
    near_edge = jnp.where(first, beside[128:224].astype(F32), beside[32:128].astype(F32))
    far_edge = jnp.where(ends, outer[64:160].astype(F32), opposite[64:160].astype(F32))
    return jnp.where(first, far_edge, near_edge), jnp.where(first, near_edge, far_edge)


def strips(mine, beside, opposite, outer):
    first = (mine & 1) == 0
    low = mine < 2
    inner, outside = opposite[0:64].astype(F32), outer[0:64].astype(F32)
    prev = jnp.where(low, outside, inner)
    follow = jnp.where(low, inner, outside)
    partner = beside[0:32].astype(F32)
    before2 = jnp.where(first, prev[0:32], prev[32:64])
    before = jnp.where(first, prev[32:64], partner)
    after = jnp.where(first, partner, follow[0:32])
    after2 = jnp.where(first, follow[0:32], follow[32:64])
    return before2, before, after, after2


def sort_terms(place, received, message, rows_named):
    spot = place[0]
    lines = lax.broadcasted_iota(jnp.int32, (4 * SLAB, LANES), 0)
    line_row = (lines >> 6) * 512 + spot * 32 - 16 + (lines & (SLAB - 1))
    sums = [None] * 4
    tile = lax.broadcasted_iota(jnp.int32, (ROWS, LANES), 0)
    head, last = tile == 0, tile == ROWS - 1
    for q in range(4):
        coded = sum(received[4 * q + i, 128:144, :].astype(F32) for i in range(4))
        named = coded[0:1] * 64.0 + coded[1:2]
        rows_named[q : q + 1, :] = named
        picks = jnp.where(line_row == named.astype(jnp.int32), 1.0, 0.0).astype(BF)
        for f in range(4):
            some = received[4 * q : 4 * q + 4, f * 32 : f * 32 + 32, :].reshape(LANES, LANES)
            part = jnp.dot(picks, some, preferred_element_type=F32)
            sums[f] = part if sums[f] is None else sums[f] + part
    for c in range(4):
        for h in range(2):
            base = c * SLAB + 16 + h * 16
            heat, rain, push_e, push_n = (
                sums[f][base - 16 : base + 32] for f in range(4)
            )
            pieces = [
                jnp.where(head, south(heat[8:16]), rain[0:8]),
                rain[8:40],
                jnp.where(last, north(heat[32:40]), rain[40:48]),
                push_e,
                push_n,
                heat[16:32],
            ]
            message[c * 2 + h] = jnp.concatenate(pieces, axis=0).astype(BF)


def add_up(received, total):
    some = received[0].astype(F32)
    for p in range(1, 8):
        some = some + received[p].astype(F32)
    total[...] = some


def first_step(quarter, tracer, mixing, own, beside, opposite, outer, base, reply, factors, halo, mix_halo, work):
    mine = quarter[0]
    before, after = edge_sides(mine, beside, opposite, outer)
    _, wet_before, wet_after, _ = (strip[24:32] for strip in strips(mine, beside, opposite, outer))
    halo[...] = jnp.zeros_like(halo)
    mix_halo[...] = jnp.zeros_like(mix_halo)
    halo[pl.ds(0, LEVELS, stride=ROWS), :] = after[0:32]
    halo[pl.ds(1, LEVELS, stride=ROWS), :] = after[32:64]
    halo[pl.ds(6, LEVELS, stride=ROWS), :] = before[0:32]
    halo[pl.ds(7, LEVELS, stride=ROWS), :] = before[32:64]
    mix_halo[pl.ds(0, LEVELS, stride=ROWS), :] = after[64:96]
    mix_halo[pl.ds(7, LEVELS, stride=ROWS), :] = before[64:96]
    lower = lax.broadcasted_iota(jnp.int32, (ROWS, LANES), 0) < 4
    wet = jnp.concatenate(
        [own[24:32], jnp.where(lower, wet_after, wet_before)], axis=0
    )
    face_e = wet * east(wet)
    face_n = wet * north(wet)
    face_w = west(face_e)
    face_s = south(face_n)

    def level(ref, own, l):
        return jnp.concatenate([own[l], ref[l * ROWS : (l + 1) * ROWS, :]], axis=0)

    zero = jnp.zeros((2 * ROWS, LANES), F32)
    over, ratio, solved, gone = zero, zero, zero, zero
    for l in range(LEVELS):
        t = level(halo, tracer, l)
        explicit = t + spread_gain * (
            face_e * (east(t) - t)
            - face_w * (t - west(t))
            + face_n * (north(t) - t)
            - face_s * (t - south(t))
        )
        under = level(mix_halo, mixing, l) if l < LEVELS - 1 else zero
        inverse = 1.0 / (1.0 + under + over * (1.0 - ratio))
        carry = over * inverse
        ratio = under * inverse
        solved = explicit * inverse + carry * solved
        gone = carry * gone if l else inverse
        factors[0, l] = inverse[0:ROWS]
        factors[1, l] = carry[0:ROWS]
        factors[2, l] = ratio[0:ROWS]
        work[l] = ratio
        base[l] = solved
        reply[l] = gone
        over = under
    for l in range(LEVELS - 2, -1, -1):
        solved = base[l] + work[l] * solved
        gone = reply[l] + work[l] * gone
        base[l] = solved
        reply[l] = gone


def ocean(
    quarter, flux, flux_beside, own, beside, opposite, outer, base, reply, factors,
    tracer_out, height_out, message, work,
):
    mine = quarter[0]
    before2, before, after, after2 = strips(mine, beside, opposite, outer)

    def ring(i, own):
        r = slice(i * ROWS, (i + 1) * ROWS)
        return jnp.concatenate([own, after[r], after2[r], before2[r], before[r]], axis=0)

    first = (mine & 1) == 0
    total = flux[...] + flux_beside[...]

    def window(start):
        blocks = [total[start + i * ROWS : start + (i + 1) * ROWS] for i in range(6)]
        parts = [jnp.where(first, blocks[i], blocks[i + 1]) for i in (2, 3, 4, 0, 1)]
        return jnp.concatenate(parts, axis=0)

    wet = ring(3, own[24:32])
    rain = fresh_gain * window(0) * wet
    h = ring(0, own[0:8])
    face_e = wet * east(wet)
    face_n = wet * north(wet)
    flow_e = wave_gain * ring(1, own[8:16])
    flow_n = wave_gain * ring(2, own[16:24])
    push_e = (wave_gain * stress_gain) * window(48)
    push_n = (wave_gain * stress_gain) * window(96)
    face_w, flow_w, push_w = west(face_e), west(flow_e), west(push_e)
    face_s, flow_s, push_s = south(face_n), south(flow_n), south(push_n)
    slope = wave_gain * wave_gain
    slope_e, slope_w, slope_n, slope_s = (
        slope * face for face in (face_e, face_w, face_n, face_s)
    )
    for turn in range(NSTEP * NSUB):
        if turn == NSUB:

            def inner(v):
                return jnp.concatenate([v[0:16], v[32:40]], axis=0)

            h, flow_e, flow_w, flow_n, flow_s = map(inner, (h, flow_e, flow_w, flow_n, flow_s))
            face_e, face_w, face_n, face_s = map(inner, (face_e, face_w, face_n, face_s))
            push_e, push_w, push_n, push_s = map(inner, (push_e, push_w, push_n, push_s))
            slope_e, slope_w, slope_n, slope_s = map(inner, (slope_e, slope_w, slope_n, slope_s))
            rain = inner(rain)
        flow_e = face_e * (flow_e + push_e) - slope_e * (east(h) - h)
        flow_w = face_w * (flow_w + push_w) - slope_w * (h - west(h))
        flow_n = face_n * (flow_n + push_n) - slope_n * (north(h) - h)
        flow_s = face_s * (flow_s + push_s) - slope_s * (h - south(h))
        h = (h + rain) - ((flow_e - flow_w) + (flow_n - flow_s))
    height_out[...] = h[0:ROWS]

    wet16 = jnp.concatenate([wet[0:ROWS], jnp.where(
        lax.broadcasted_iota(jnp.int32, (ROWS, LANES), 0) < 4, wet[8:16], wet[32:40])], axis=0)
    tile = lax.broadcasted_iota(jnp.int32, (ROWS, LANES), 0)
    heat_low, heat_high = total[144:152], total[152:160]
    after_heat = jnp.where(first, heat_high, south(total[40:48]))
    before_heat = jnp.where(first, north(total[0:8]), heat_low)
    halo_heat = jnp.where(tile == 0, after_heat, jnp.where(tile == ROWS - 1, before_heat, 0.0))
    heat = jnp.concatenate([jnp.where(first, heat_low, heat_high), halo_heat], axis=0)
    warm = heating_gain * heat * wet16
    fe, fw, fn, fs = face_e[0:ROWS], face_w[0:ROWS], face_n[0:ROWS], face_s[0:ROWS]
    solved = None
    for l in range(LEVELS):
        both = base[l] + reply[l] * warm
        t = both[0:ROWS]
        explicit = t + spread_gain * (
            fe * (east(t) - t)
            - fw * (t - west(t))
            + fn * (north(both)[0:ROWS] - t)
            - fs * (t - south(both)[0:ROWS])
        )
        if l == 0:
            explicit = explicit + warm[0:ROWS]
            solved = explicit * factors[0, l]
        else:
            solved = explicit * factors[0, l] + factors[1, l] * solved
        work[l] = solved
    tracer_out[LEVELS - 1] = solved
    for l in range(LEVELS - 2, -1, -1):
        solved = work[l] + factors[2, l] * solved
        tracer_out[l] = solved
    top = jnp.concatenate([solved, h[0:ROWS]], axis=0).astype(BF)
    for p in range(GROUP):
        message[p] = top


def answer(place, rows_named, received, message):
    spot = place[0]
    have = received[...].reshape(GROUP * 16, LANES)
    lines = lax.broadcasted_iota(jnp.int32, (GROUP * 16, LANES), 0)
    line_row = (lines >> 6) * 512 + spot * 32 + ((lines >> 4) & 3) * ROWS + (lines & 7)
    second = (lines & 8) != 0
    for q in range(4):
        named = rows_named[q : q + 1, :].astype(jnp.int32)
        same = line_row == named
        for f in range(2):
            picks = jnp.where(same & (second == bool(f)), 1.0, 0.0).astype(BF)
            out = lax.dot_general(
                picks, have, (((0,), (0,)), ((), ())), preferred_element_type=F32
            ).astype(BF)
            message[4 * q : 4 * q + 4, f * 32 : f * 32 + 32, :] = out.reshape(4, 32, LANES)


def finish(received, weights, tracer, height, out_far, tracer_out, height_out, flat, out, done):
    saves = [
        pltpu.make_async_copy(tracer, tracer_out, done.at[0]),
        pltpu.make_async_copy(height, height_out, done.at[1]),
    ]
    for save in saves:
        save.start()
    total = received[0].astype(F32)
    for p in range(1, GROUP):
        total = total + received[p].astype(F32)
    flat[...] = total
    for s in range(0, 8, 2):
        answer = None
        for k in (0, 2):
            left = jnp.concatenate(
                [
                    jnp.concatenate(
                        [flat[pl.ds(i * 4 + j, 2, stride=TERMS), :] for j in (k, k + 1)], axis=1
                    )
                    for i in (s, s + 1)
                ],
                axis=0,
            ).astype(BF)
            right = jnp.concatenate(
                [
                    jnp.concatenate([weights[i, k], weights[i, k + 1]], axis=1)
                    for i in (s, s + 1)
                ],
                axis=0,
            )
            part = lax.dot_general(
                left, right, (((1,), (1,)), ((), ())), preferred_element_type=F32
            )
            answer = part if answer is None else answer + part
        out[:, s * LANES : (s + 1) * LANES] = answer[0:2, 0:LANES].astype(BF)
        out[:, (s + 1) * LANES : (s + 2) * LANES] = answer[2:4, LANES:].astype(BF)
    last = pltpu.make_async_copy(out, out_far, done.at[2])
    last.start()
    for save in (*saves, last):
        save.wait()


def shards(airside, matrices, latitude, tracer, mixing, height, flow, marine):
    spot = lax.axis_index(PLANE).astype(jnp.int32)
    turn = lax.axis_index(("h", "k")).astype(jnp.int32)
    place, quarter = spot.reshape(1), turn.reshape(1)
    count = lax.axis_size(ALL)

    leaving, own, weights, tracer, mixing, first = call(
        prepare,
        (
            inside((224, LANES), BF),
            inside((32, LANES), F32),
            inside((8, 4, LANES, LANES), BF),
            inside((LEVELS, ROWS, LANES), F32),
            inside((LEVELS - 1, ROWS, LANES), F32),
            shaped((GROUP, 144, LANES), BF),
        ),
        [smem] + [far] * 8,
        [
            pltpu.VMEM((ROWS, LANES), jnp.int32),
            pltpu.VMEM((4, 8), jnp.int32),
            pltpu.VMEM((4, 8 * LANES), BF),
            pltpu.VMEM((4 * TERMS, LANES), F32),
            pltpu.VMEM((144, LANES), BF),
            pltpu.SemaphoreType.DMA((16,)),
            pltpu.SemaphoreType.DMA((16,)),
        ],
        out_specs=(vmem,) * 5 + (far,),
        room=60 * 1024,
    )(
        place, tracer, mixing, height, flow, marine,
        latitude[0].T, airside[0], matrices[0],
    )
    leaving, own, weights, tracer, mixing = map(near, (leaving, own, weights, tracer, mixing))
    first = near(lax.all_to_all(first, PLANE, 0, 0, tiled=True))
    flip = [(i, i ^ 1) for i in range(count)]
    pairs = []
    for i in range(count):
        j = i + 2 if i & 2 else i - 2
        if 0 <= j < count:
            pairs.append((i, j))
    beside = near(lax.ppermute(leaving, ALL, flip))
    across, outward = call(
        chip_edges, (inside((160, LANES), BF), inside((160, LANES), BF)), [smem] + [vmem] * 2
    )(quarter, leaving, beside)
    opposite = near(lax.ppermute(near(across), ALL, [(i, i ^ 2) for i in range(count)]))
    outer = near(lax.ppermute(near(outward), ALL, pairs))

    second, rows_named = call(
        sort_terms, (inside((8, 160, LANES), BF), inside((ROWS, LANES), F32)), [smem, vmem]
    )(place, first)
    rows_named = near(rows_named)
    second = near(lax.all_to_all(second, ("c", "h"), 0, 0, tiled=True))
    flux = near(call(add_up, inside((160, LANES), F32), [vmem])(second))
    flux_beside = near(lax.ppermute(flux, ALL, flip))

    base, reply, factors = call(
        first_step,
        (
            inside((LEVELS, 2 * ROWS, LANES), F32),
            inside((LEVELS, 2 * ROWS, LANES), F32),
            inside((3, LEVELS, ROWS, LANES), F32),
        ),
        [smem] + [vmem] * 6,
        [
            pltpu.VMEM((LEVELS * ROWS, LANES), F32),
            pltpu.VMEM((LEVELS * ROWS, LANES), F32),
            pltpu.VMEM((LEVELS, 2 * ROWS, LANES), F32),
        ],
    )(quarter, tracer, mixing, own, beside, opposite, outer)

    tracer_new, height_new, third = call(
        ocean,
        (
            inside((LEVELS, ROWS, LANES), F32),
            inside((ROWS, LANES), F32),
            inside((GROUP, 16, LANES), BF),
        ),
        [smem] + [vmem] * 9,
        [pltpu.VMEM((LEVELS, ROWS, LANES), F32)],
    )(quarter, flux, flux_beside, own, beside, opposite, outer, near(base), near(reply), near(factors))
    third = near(lax.all_to_all(third, LINE, 0, 0, tiled=True))

    fourth = call(
        answer, inside((GROUP, 64, LANES), BF), [smem, vmem, vmem]
    )(place, rows_named, third)
    fourth = near(lax.all_to_all(fourth, PLANE, 0, 0, tiled=True))

    returned, tracer_new, height_new = call(
        finish,
        (
            shaped((2, 8 * LANES), BF),
            shaped((LEVELS, ROWS, LANES), F32),
            shaped((ROWS, LANES), F32),
        ),
        [vmem] * 4,
        [
            pltpu.VMEM((2 * TERMS, LANES), F32),
            pltpu.VMEM((2, 8 * LANES), BF),
            pltpu.SemaphoreType.DMA((3,)),
        ],
        out_specs=(far, far, far),
    )(fourth, weights, near(tracer_new), near(height_new))
    return tracer_new, height_new, returned[None]


def solution(mesh):
    split = Mesh(mesh.devices.reshape(4, 4, 4, 2, 2), ALL)
    dom = ("y", "x", "h", "k")
    return jax.shard_map(
        shards,
        mesh=split,
        in_specs=(
            P("c", None, dom),
            P("c", dom, None, None, None),
            P("c", dom, None),
            P(None, ALL, None),
            P(None, ALL, None),
            P(ALL, None),
            P(None, ALL, None),
            P(ALL, None),
        ),
        out_specs=(P(None, ALL, None), P(ALL, None), P("c", None, dom)),
        check_vma=False,
    )
```
